32 devices in a mesh: group: 2 (over y), sector: 16 (over z, x, core).
Axes of the slice: x: 2, y: 2, z: 4, core: 2. Of those that a mesh axis runs over, the one named last changes fastest.
Arguments:
- wavefunction: bfloat16 [16, 512, 512], P('sector'), may hold values from -6 to 6
- left_factors: bfloat16 [6, 512, 512], P('group'), may hold values from -0.125 to 0.125
- right_factors: bfloat16 [6, 512, 512], P('group'), may hold values from -0.125 to 0.125
- term_list: int32 [128, 3], P(('group', 'sector')), may hold values from 0 to 2, as said below
- term_counts: int32 [32], P(('group', 'sector')), may hold values from 1 to 4, as said below
- sector_sizes: int32 [16], replicated, may hold values from 128 to 512, as said below
Outputs:
- product_wave: bfloat16 [16, 512, 512], P('sector', 'group')
The draws below stay inside these ranges and needn't reach their ends.
Inputs may be any that keep to these rules, and one draw needn't show every extreme that they name: `term_list`: column 0 lies in 0 to 2 and never points outside the sectors (no 0 for sector 0, no 2 for sector 16 - 1); columns 1 and 2 name factors 0 to 2 of the slot's own group. `term_counts`: each owner has 1 or 4 live slots; some owner has 4. `sector_sizes`: sector 0 is full.
All inputs are finite; a program needn't handle non-finite values.
Results may differ from the reference program's by a relative error of at most 0.0049.
Values may be sent and summed in bfloat16 or wider, within the bound.
No kernel may reach another device: no remote copies, remote signals or barrier semaphores. Data moves between devices by JAX's collectives and lax.ppermute only.
A program may use at most 64 MiB of HBM per device.

```python
import jax
import jax.numpy as jnp
from jax import lax

B = 512
OPS = 3
TERM_DEV = 4
SECTORS = 16
GROUP_FACTORS = 6
N_GROUP = 2
N_SECTOR = 16


def draw_term_list(key, part):
    count = N_GROUP * N_SECTOR * TERM_DEV
    first, second, third = jax.random.split(jax.random.fold_in(key, 11), 3)
    numbers = jnp.arange(count, dtype=jnp.int32)
    sector_here = numbers // TERM_DEV % N_SECTOR
    lowest = (sector_here == 0).astype(jnp.int32)
    highest = 3 - (sector_here == N_SECTOR - 1).astype(jnp.int32)
    change = jax.random.randint(first, (count,), lowest, highest, dtype=jnp.int32)
    left_pick = jax.random.randint(second, (count,), 0, OPS, dtype=jnp.int32)
    right_pick = jax.random.randint(third, (count,), 0, OPS, dtype=jnp.int32)
    return jnp.stack([change, left_pick, right_pick], axis=1).astype(jnp.int32)


def draw_term_counts(key, part):
    owners = N_GROUP * N_SECTOR
    picks = jax.random.randint(jax.random.fold_in(key, 23), (owners,), 0, 4, dtype=jnp.int32)
    counted = jnp.where(picks == 0, TERM_DEV, 1).astype(jnp.int32)
    return counted.at[0].set(TERM_DEV)


def draw_sector_sizes(key, part):
    sizes = jax.random.randint(jax.random.fold_in(key, 37), (N_SECTOR,), B // 4, B + 1, dtype=jnp.int32)
    return sizes.at[0].set(B)


def levels(own_key, extent, cuts, smallest, high):
    level = 1.0
    for dim, parts in cuts:
        steps = jax.random.uniform(jax.random.fold_in(jax.random.fold_in(own_key, 6), dim), (parts,), jnp.float32, smallest / len(cuts), high / len(cuts))
        level = level * jnp.repeat(jnp.exp(steps), extent[dim] // parts).reshape((-1,) + (1,) * (len(extent) - 1 - dim))
    return level


def normal_values(key, extent, spread, most, pieces=(), kind=jnp.bfloat16):
    result = jax.random.normal(key, extent, jnp.float32) * spread
    if len(pieces) > 0:
        result = levels(key, extent, pieces, -0.22, 0.18) * result
    return jnp.clip(result, min=-most, max=most).astype(kind)


def setup_inputs(seed: int = 0) -> dict:
    keys = jax.random.split(jax.random.key(seed), 7)
    wavefunction = normal_values(keys[0], (SECTORS, B, B), 1.0, 6.0, ((0, 16),))
    left_factors = normal_values(keys[1], (GROUP_FACTORS, B, B), (4 * B) ** -0.5, 0.125, ((0, 2),))
    right_factors = normal_values(keys[2], (GROUP_FACTORS, B, B), (4 * B) ** -0.5, 0.125, ((0, 2),))
    term_list = draw_term_list(jax.random.fold_in(keys[6], 71), 0)
    term_counts = draw_term_counts(jax.random.fold_in(keys[6], 71), 0)
    sector_sizes = draw_sector_sizes(jax.random.fold_in(keys[6], 71), 0)
    return dict(wavefunction=wavefunction, left_factors=left_factors, right_factors=right_factors, term_list=term_list, term_counts=term_counts, sector_sizes=sector_sizes)


def block_mask(size, positions):
    keep = positions < size
    return (keep[:, None] & keep[None, :]).astype(jnp.bfloat16)


def forward_term(left_factor, source, right_factor):
    middle = jnp.dot(left_factor, source, preferred_element_type=jnp.float32).astype(jnp.bfloat16)
    return jnp.dot(middle, right_factor, preferred_element_type=jnp.float32)


def adjoint_term(left_factor, target, right_factor):
    middle = lax.dot_general(left_factor, target, (((0,), (0,)), ((), ())), preferred_element_type=jnp.float32).astype(jnp.bfloat16)
    return lax.dot_general(middle, right_factor, (((1,), (1,)), ((), ())), preferred_element_type=jnp.float32)


def reference(wavefunction, left_factors, right_factors, term_list, term_counts, sector_sizes):
    positions = jnp.arange(B, dtype=jnp.int32)
    masks = jax.vmap(lambda size: block_mask(size, positions))(sector_sizes)
    clean = wavefunction * masks

    def one_slot(totals, number):
        device = number // TERM_DEV
        slot_index = number % TERM_DEV
        group_index = device // N_SECTOR
        sector_here = device % N_SECTOR
        record = term_list[number]
        target = sector_here + record[0] - 1

        def work(totals):
            left_factor = left_factors[group_index * OPS + record[1]]
            right_factor = right_factors[group_index * OPS + record[2]]
            forward_part = forward_term(left_factor, clean[sector_here], right_factor)
            backward_part = adjoint_term(left_factor, clean[target], right_factor)
            totals = totals.at[target].add(forward_part)
            return totals.at[sector_here].add(backward_part)

        def skip(totals):
            return totals

        return lax.cond(slot_index < term_counts[device], work, skip, totals), None

    start = jnp.zeros((N_SECTOR, B, B), jnp.float32)
    totals, unused = lax.scan(one_slot, start, jnp.arange(term_list.shape[0], dtype=jnp.int32))
    return (masks.astype(jnp.float32) * totals).astype(jnp.bfloat16)
```

```python
import functools

import jax
import jax.numpy as jnp
from jax import lax
from jax.experimental import pallas as pl
from jax.experimental.pallas import tpu as pltpu
from jax.sharding import PartitionSpec as P

F32 = jnp.float32
BF16 = jnp.bfloat16
VMEM = pl.BlockSpec(memory_space=pltpu.VMEM)
SMEM = pl.BlockSpec(memory_space=pltpu.SMEM)
PARAMS = pltpu.CompilerParams(vmem_limit_bytes=20 * 1024 * 1024)


def dot(a, b, ca, cb):
    return lax.dot_general(a, b, (((ca,), (cb,)), ((), ())), preferred_element_type=F32)


def swap_pairs(size, odd_first):
    pairs = []
    for low in range(1 if odd_first else 0, size - 1, 2):
        pairs += [(low, low + 1), (low + 1, low)]
    return pairs


def record(ref, k):
    return ref[3 * k], ref[3 * k + 1], ref[3 * k + 2]


def masked(block, size):
    rows = lax.broadcasted_iota(jnp.int32, block.shape, 0)
    cols = lax.broadcasted_iota(jnp.int32, block.shape, 1)
    return jnp.where((rows < size) & (cols < size), block, jnp.zeros_like(block))


def forward(acc, rows, left, source, right):
    middle = dot(left[rows, :], source, 1, 0).astype(BF16)
    acc[...] += dot(middle, right[...], 1, 0)


def adjoint(acc, cols, left, source, right):
    middle = dot(left[:, cols], source, 0, 0).astype(BF16)
    acc[...] += dot(middle, right[...], 1, 1)


def live_terms(codes, slots, here, want, action):
    for k in range(slots):
        change, left, right = record(codes, k)
        live = k < codes[3 * slots]

        @pl.when(live & (here + change - 1 == want))
        def _():
            action(left, right)


def near_kernel(slots, own_codes, partner_codes, sizes, own, partner, left, right, out, own_clean, partner_clean):
    here = lax.axis_index("sector")
    friend = here + 1 - 2 * (here % 2)
    own_clean[...] = masked(own[0], sizes[here])
    partner_clean[...] = masked(partner[0], sizes[jnp.clip(friend, 0, sizes.shape[0] - 1)])
    out[...] = jnp.zeros_like(out)
    every = slice(None)

    def self_term(l, r):
        forward(out, every, left.at[l], own_clean[...], right.at[r])
        adjoint(out, every, left.at[l], own_clean[...], right.at[r])

    live_terms(own_codes, slots, here, here, self_term)
    live_terms(own_codes, slots, here, friend,
               lambda l, r: adjoint(out, every, left.at[l], partner_clean[...], right.at[r]))
    live_terms(partner_codes, slots, friend, here,
               lambda l, r: forward(out, every, left.at[l], partner_clean[...], right.at[r]))


def far_kernel(slots, share, mine, own_codes, cross_codes, sizes, cross, left, right, near, out, clean, acc):
    here = lax.axis_index("sector")
    group = lax.axis_index("group")
    other = here - 1 + 2 * (here % 2)
    clean[...] = masked(cross[0], sizes[jnp.clip(other, 0, sizes.shape[0] - 1)])

    def run(rows):
        acc[...] = near[rows, :]
        live_terms(own_codes, slots, here, other,
                   lambda l, r: adjoint(acc, rows, left.at[l], clean[...], right.at[r]))
        live_terms(cross_codes, slots, other, here,
                   lambda l, r: forward(acc, rows, left.at[l], clean[...], right.at[r]))
        out[...] = acc[...].astype(out.dtype)

    if share == near.shape[0]:
        run(slice(None))
        return
    for g in range(near.shape[0] // share):
        @pl.when((group == g) == mine)
        def _():
            run(slice(g * share, (g + 1) * share))


def last_kernel(share, sizes, kept, got, out):
    here = lax.axis_index("sector")
    group = lax.axis_index("group")
    total = kept[...]
    for i in range(got.shape[0]):
        total = total + got[i].astype(F32)
    rows = lax.broadcasted_iota(jnp.int32, total.shape, 0) + group * share
    cols = lax.broadcasted_iota(jnp.int32, total.shape, 1)
    size = sizes[here]
    out[0] = jnp.where((rows < size) & (cols < size), total, 0.0).astype(BF16)


def shards(wavefunction, left_factors, right_factors, term_list, term_counts, sector_sizes):
    width = wavefunction.shape[1]
    groups = lax.axis_size("group")
    sectors = lax.axis_size("sector")
    share = width // groups
    slots = term_list.shape[0]
    near_swap = swap_pairs(sectors, False)
    far_swap = swap_pairs(sectors, True)
    codes = jnp.concatenate([term_list.reshape(-1), term_counts])
    cross = lax.ppermute(wavefunction, "sector", far_swap)
    partner = lax.ppermute(wavefunction, "sector", near_swap)
    partner_codes = lax.ppermute(codes, "sector", near_swap)
    cross_codes = lax.ppermute(codes, "sector", far_swap)
    block = pltpu.VMEM((width, width), BF16)
    near = pl.pallas_call(
        functools.partial(near_kernel, slots),
        out_shape=jax.ShapeDtypeStruct((width, width), F32),
        in_specs=[SMEM, SMEM, SMEM, VMEM, VMEM, VMEM, VMEM],
        out_specs=VMEM,
        scratch_shapes=[block, block],
        compiler_params=PARAMS,
        name="near",
    )(codes, partner_codes, sector_sizes, wavefunction, partner, left_factors, right_factors)

    def far(rows, mine, dtype):
        return pl.pallas_call(
            functools.partial(far_kernel, slots, rows, mine),
            out_shape=jax.ShapeDtypeStruct((rows, width), dtype),
            in_specs=[SMEM, SMEM, SMEM, VMEM, VMEM, VMEM, VMEM],
            out_specs=VMEM,
            scratch_shapes=[block, pltpu.VMEM((rows, width), F32)],
            compiler_params=PARAMS,
            name="far_mine" if mine else "far_theirs",
        )(codes, cross_codes, sector_sizes, cross, left_factors, right_factors, near)

    if groups == 2 and share % 128 == 0:
        theirs = far(share, False, BF16)
        got = lax.ppermute(theirs, "group", [(0, 1), (1, 0)])[None]
        kept = far(share, True, F32)
    else:
        whole = far(width, True, F32)
        group = lax.axis_index("group")
        kept = lax.dynamic_slice_in_dim(whole, group * share, share, 0)
        parts = []
        for hop in range(1, groups):
            target = (group + hop) % groups
            part = lax.dynamic_slice_in_dim(whole, target * share, share, 0).astype(BF16)
            parts.append(lax.ppermute(part, "group", [(i, (i + hop) % groups) for i in range(groups)]))
        got = jnp.stack(parts) if parts else jnp.zeros((1, share, width), BF16)
    return pl.pallas_call(
        functools.partial(last_kernel, share),
        out_shape=jax.ShapeDtypeStruct((1, share, width), BF16),
        in_specs=[SMEM, VMEM, VMEM],
        out_specs=VMEM,
        compiler_params=PARAMS,
        name="last",
    )(sector_sizes, kept, got)


def solution(mesh):
    return jax.shard_map(
        shards,
        mesh=mesh,
        in_specs=(
            P("sector", None, None),
            P("group", None, None),
            P("group", None, None),
            P(("group", "sector"), None),
            P(("group", "sector")),
            P(),
        ),
        out_specs=P("sector", "group", None),
        check_vma=False,
    )
```

```python
import functools

import jax
import jax.numpy as jnp
from jax import lax
from jax.experimental import pallas as pl
from jax.experimental.pallas import tpu as pltpu
from jax.sharding import PartitionSpec as P

F32 = jnp.float32
BF16 = jnp.bfloat16
VMEM = pl.BlockSpec(memory_space=pltpu.VMEM)
SMEM = pl.BlockSpec(memory_space=pltpu.SMEM)
HBM = pl.BlockSpec(memory_space=pltpu.HBM)
PARAMS = pltpu.CompilerParams(vmem_limit_bytes=16 * 1024 * 1024)


def dot(a, b, ca, cb):
    return lax.dot_general(a, b, (((ca,), (cb,)), ((), ())), preferred_element_type=F32)


def forward(acc, left, source, right):
    middle = dot(left[...], source[...], 1, 0).astype(BF16)
    acc[...] += dot(middle, right[...], 1, 0)


def adjoint(acc, left, source, right):
    middle = dot(left[...], source[...], 0, 0).astype(BF16)
    acc[...] += dot(middle, right[...], 1, 1)


def friend_of(sector):
    return sector + 1 - 2 * (sector % 2)


def other_of(sector):
    return sector - 1 + 2 * (sector % 2)


def masked(block, size):
    rows = lax.broadcasted_iota(jnp.int32, block.shape, 0)
    cols = lax.broadcasted_iota(jnp.int32, block.shape, 1)
    return jnp.where((rows < size) & (cols < size), block, jnp.zeros_like(block))


def live_terms(codes, owner, want, action):
    for k in range(codes.shape[0]):
        @pl.when(owner + codes[k, 0] - 2 == want)
        def _():
            action(codes[k, 1] - 1, codes[k, 2] - 1)


def row_shares(acc, groups):
    share = acc.shape[0] // groups
    group = lax.axis_index("group")
    return [acc[pl.ds(pl.multiple_of((group + hop) % groups * share, share), share), :] for hop in range(groups)]


def far_kernel(groups, own_codes, other_codes, sizes, own_hbm, left_hbm, right_hbm, *refs):
    parts, (left, right, clean, acc, own, sems) = refs[:groups], refs[groups:]
    here = lax.axis_index("sector")
    other = other_of(here)
    count = left.shape[0]
    copies = [pltpu.make_async_copy(own_hbm.at[0], own, sems.at[2 * count])]
    for i in range(count):
        copies.append(pltpu.make_async_copy(left_hbm.at[i], left.at[i], sems.at[i]))
        copies.append(pltpu.make_async_copy(right_hbm.at[i], right.at[i], sems.at[count + i]))
    for copy in copies:
        copy.start()
    acc[...] = jnp.zeros_like(acc)
    copies[0].wait()
    clean[...] = masked(own[...], sizes[here])
    for copy in copies[1:]:
        copy.wait()
    live_terms(own_codes, here, other, lambda l, r: forward(acc, left.at[l], clean, right.at[r]))
    live_terms(other_codes, other, here, lambda l, r: adjoint(acc, left.at[l], clean, right.at[r]))
    for part, rows in zip(parts, row_shares(acc, groups)):
        part[...] = rows.astype(BF16)


def near_kernel(groups, own_codes, friend_codes, sizes, clean, friend_block, left, right, *refs):
    kept, parts, (friend_clean, acc) = refs[0], refs[1:groups], refs[groups:]
    here = lax.axis_index("sector")
    friend = friend_of(here)
    friend_clean[...] = masked(friend_block[0], sizes[jnp.minimum(friend, sizes.shape[0] - 1)])
    acc[...] = jnp.zeros_like(acc)

    def self_term(l, r):
        forward(acc, left.at[l], clean, right.at[r])
        adjoint(acc, left.at[l], clean, right.at[r])

    live_terms(own_codes, here, here, self_term)
    live_terms(own_codes, here, friend, lambda l, r: adjoint(acc, left.at[l], friend_clean, right.at[r]))
    live_terms(friend_codes, friend, here, lambda l, r: forward(acc, left.at[l], friend_clean, right.at[r]))
    shares = row_shares(acc, groups)
    kept[...] = shares[0]
    for part, rows in zip(parts, shares[1:]):
        part[...] = rows.astype(BF16)


def last_kernel(sizes, kept, *refs):
    got, out = refs[:-1], refs[-1]
    share = kept.shape[0]
    total = kept[...]
    for part in got:
        total = total + part[...].astype(F32)
    rows = lax.broadcasted_iota(jnp.int32, total.shape, 0) + lax.axis_index("group") * share
    cols = lax.broadcasted_iota(jnp.int32, total.shape, 1)
    size = sizes[lax.axis_index("sector")]
    out[0] = jnp.where((rows < size) & (cols < size), total, 0.0).astype(BF16)


def shards(wavefunction, left_factors, right_factors, term_list, term_counts, sector_sizes):
    width = wavefunction.shape[1]
    groups = lax.axis_size("group")
    sectors = lax.axis_size("sector")
    share = width // groups
    slots = term_list.shape[0]
    factors = left_factors.shape
    friends = [(s, friend_of(s)) for s in range(sectors) if friend_of(s) < sectors]
    others = [(s, other_of(s)) for s in range(sectors) if 0 <= other_of(s) < sectors]

    def onward(hop, pairs):
        return [(g * sectors + s, (g + hop) % groups * sectors + t) for g in range(groups) for s, t in pairs]

    live = jnp.arange(slots, dtype=jnp.int32)[:, None] < term_counts
    codes = jnp.where(live, term_list + 1, 0)
    other_codes = lax.ppermute(codes, "sector", others)
    friend_codes = lax.ppermute(codes, "sector", friends)
    friend_block = lax.ppermute(wavefunction, "sector", friends)
    part = jax.ShapeDtypeStruct((share, width), BF16)
    block = pltpu.VMEM((width, width), BF16)
    total = pltpu.VMEM((width, width), F32)
    *far_parts, left, right, clean = pl.pallas_call(
        functools.partial(far_kernel, groups),
        out_shape=[part] * groups + [
            jax.ShapeDtypeStruct(factors, BF16),
            jax.ShapeDtypeStruct(factors, BF16),
            jax.ShapeDtypeStruct((width, width), BF16),
        ],
        in_specs=[SMEM, SMEM, SMEM, HBM, HBM, HBM],
        out_specs=[VMEM] * (groups + 3),
        scratch_shapes=[total, block, pltpu.SemaphoreType.DMA((2 * factors[0] + 1,))],
        compiler_params=PARAMS,
        name="far",
    )(codes, other_codes, sector_sizes, wavefunction, left_factors, right_factors)
    got = []
    for hop in list(range(1, groups)) + [0]:
        got.append(lax.ppermute(far_parts[hop], ("group", "sector"), onward(hop, others)))
    kept, *near_parts = pl.pallas_call(
        functools.partial(near_kernel, groups),
        out_shape=[jax.ShapeDtypeStruct((share, width), F32)] + [part] * (groups - 1),
        in_specs=[SMEM, SMEM, SMEM, VMEM, VMEM, VMEM, VMEM],
        out_specs=[VMEM] * groups,
        scratch_shapes=[block, total],
        compiler_params=PARAMS,
        name="near",
    )(codes, friend_codes, sector_sizes, clean, friend_block, left, right)
    for hop in range(1, groups):
        got.append(lax.ppermute(near_parts[hop - 1], "group", [(g, (g + hop) % groups) for g in range(groups)]))
    return pl.pallas_call(
        last_kernel,
        out_shape=jax.ShapeDtypeStruct((1, share, width), BF16),
        in_specs=[SMEM, VMEM] + [VMEM] * len(got),
        out_specs=VMEM,
        compiler_params=PARAMS,
        name="last",
    )(sector_sizes, kept, *got)


def solution(mesh):
    return jax.shard_map(
        shards,
        mesh=mesh,
        in_specs=(
            P("sector", None, None),
            P("group", None, None),
            P("group", None, None),
            P(("group", "sector"), None),
            P(("group", "sector")),
            P(),
        ),
        out_specs=P("sector", "group", None),
        check_vma=False,
    )
```

```python
import functools

import jax
import jax.numpy as jnp
from jax import lax
from jax.experimental import pallas as pl
from jax.experimental.pallas import tpu as pltpu
from jax.sharding import PartitionSpec as P

F32 = jnp.float32
BF16 = jnp.bfloat16
VMEM = pl.BlockSpec(memory_space=pltpu.VMEM)
SMEM = pl.BlockSpec(memory_space=pltpu.SMEM)
HBM = pl.BlockSpec(memory_space=pltpu.HBM)
PARAMS = pltpu.CompilerParams(vmem_limit_bytes=16 * 1024 * 1024)


def dot(a, b, ca, cb):
    return lax.dot_general(a, b, (((ca,), (cb,)), ((), ())), preferred_element_type=F32)


def forward(acc, left, source, right):
    middle = dot(left[...], source[...], 1, 0).astype(BF16)
    acc[...] += dot(middle, right[...], 1, 0)


def adjoint(acc, left, source, right):
    middle = dot(left[...], source[...], 0, 0).astype(BF16)
    acc[...] += dot(middle, right[...], 1, 1)


def friend_of(sector):
    return sector + 1 - 2 * (sector % 2)


def other_of(sector):
    return sector - 1 + 2 * (sector % 2)


def masked(block, size):
    rows = lax.broadcasted_iota(jnp.int32, block.shape, 0)
    cols = lax.broadcasted_iota(jnp.int32, block.shape, 1)
    return jnp.where((rows < size) & (cols < size), block, jnp.zeros_like(block))


def live_terms(codes, owner, want, action):
    for k in range(codes.shape[0]):
        @pl.when(owner + codes[k, 0] - 2 == want)
        def _():
            action(codes[k, 1] - 1, codes[k, 2] - 1)


def near_kernel(own_codes, friend_codes, sizes, own_hbm, friend_block, left_hbm, right_hbm,
                acc, left, right, own, clean, friend_clean, sems):
    here = lax.axis_index("sector")
    friend = friend_of(here)
    count = left.shape[0]
    copies = [pltpu.make_async_copy(own_hbm.at[0], own, sems.at[2 * count])]
    for i in range(count):
        copies.append(pltpu.make_async_copy(left_hbm.at[i], left.at[i], sems.at[i]))
        copies.append(pltpu.make_async_copy(right_hbm.at[i], right.at[i], sems.at[count + i]))
    for copy in copies:
        copy.start()
    friend_clean[...] = masked(friend_block[0], sizes[jnp.minimum(friend, sizes.shape[0] - 1)])
    acc[...] = jnp.zeros_like(acc)
    copies[0].wait()
    clean[...] = masked(own[...], sizes[here])
    for copy in copies[1:]:
        copy.wait()

    def self_term(l, r):
        forward(acc, left.at[l], clean, right.at[r])
        adjoint(acc, left.at[l], clean, right.at[r])

    live_terms(own_codes, here, here, self_term)
    live_terms(own_codes, here, friend, lambda l, r: adjoint(acc, left.at[l], friend_clean, right.at[r]))
    live_terms(friend_codes, friend, here, lambda l, r: forward(acc, left.at[l], friend_clean, right.at[r]))


def far_kernel(mine, own_codes, other_codes, sizes, other_block, left, right, near, out, clean, acc):
    here = lax.axis_index("sector")
    other = other_of(here)
    share = out.shape[0]
    clean[...] = masked(other_block[0], sizes[jnp.clip(other, 0, sizes.shape[0] - 1)])

    def run(rows):
        acc[...] = near[rows, :]
        live_terms(own_codes, here, other,
                   lambda l, r: adjoint(acc, left.at[l, :, rows], clean, right.at[r]))
        live_terms(other_codes, other, here,
                   lambda l, r: forward(acc, left.at[l, rows, :], clean, right.at[r]))
        out[...] = acc[...].astype(out.dtype)

    if share == near.shape[0]:
        run(slice(None))
        return
    for g in range(near.shape[0] // share):
        @pl.when((lax.axis_index("group") == g) == mine)
        def _():
            run(slice(g * share, (g + 1) * share))


def last_kernel(sizes, kept, *refs):
    got, out = refs[:-1], refs[-1]
    share = kept.shape[0]
    total = kept[...]
    for part in got:
        total = total + part[...].astype(F32)
    rows = lax.broadcasted_iota(jnp.int32, total.shape, 0) + lax.axis_index("group") * share
    cols = lax.broadcasted_iota(jnp.int32, total.shape, 1)
    size = sizes[lax.axis_index("sector")]
    out[0] = jnp.where((rows < size) & (cols < size), total, 0.0).astype(BF16)


def shards(wavefunction, left_factors, right_factors, term_list, term_counts, sector_sizes):
    width = wavefunction.shape[1]
    groups = lax.axis_size("group")
    sectors = lax.axis_size("sector")
    share = width // groups
    slots = term_list.shape[0]
    factors = left_factors.shape
    friends = [(s, friend_of(s)) for s in range(sectors) if friend_of(s) < sectors]
    others = [(s, other_of(s)) for s in range(sectors) if 0 <= other_of(s) < sectors]
    block = pltpu.VMEM((width, width), BF16)
    hbm = functools.partial(pltpu.with_memory_space_constraint, memory_space=pltpu.HBM)

    other_block = lax.ppermute(wavefunction, "sector", others)
    friend_block = lax.ppermute(wavefunction, "sector", friends)
    live = jnp.arange(slots, dtype=jnp.int32)[:, None] < term_counts
    codes = jnp.where(live, term_list + 1, 0)
    friend_codes = lax.ppermute(codes, "sector", friends)
    other_codes = lax.ppermute(codes, "sector", others)
    near, left, right = pl.pallas_call(
        near_kernel,
        out_shape=[
            jax.ShapeDtypeStruct((width, width), F32),
            jax.ShapeDtypeStruct(factors, BF16),
            jax.ShapeDtypeStruct(factors, BF16),
        ],
        in_specs=[SMEM, SMEM, SMEM, HBM, VMEM, HBM, HBM],
        out_specs=[VMEM] * 3,
        scratch_shapes=[block, block, block, pltpu.SemaphoreType.DMA((2 * factors[0] + 1,))],
        compiler_params=PARAMS,
        name="near",
    )(codes, friend_codes, sector_sizes, hbm(wavefunction), friend_block, hbm(left_factors), hbm(right_factors))

    def far(rows, mine, dtype):
        return pl.pallas_call(
            functools.partial(far_kernel, mine),
            out_shape=jax.ShapeDtypeStruct((rows, width), dtype),
            in_specs=[SMEM, SMEM, SMEM, VMEM, VMEM, VMEM, VMEM],
            out_specs=VMEM,
            scratch_shapes=[block, pltpu.VMEM((rows, width), F32)],
            compiler_params=PARAMS,
            name="far_mine" if mine else "far_theirs",
        )(codes, other_codes, sector_sizes, other_block, left, right, near)

    hops = [[(g, (g + hop) % groups) for g in range(groups)] for hop in range(1, groups)]
    if groups == 2 and share % 128 == 0:
        theirs = far(share, False, BF16)
        got = [lax.ppermute(theirs, "group", hops[0])]
        kept = far(share, True, F32)
    else:
        whole = far(width, True, F32)
        group = lax.axis_index("group")
        kept = lax.dynamic_slice_in_dim(whole, group * share, share, 0)
        got = []
        for hop, pairs in enumerate(hops, 1):
            part = lax.dynamic_slice_in_dim(whole, (group + hop) % groups * share, share, 0)
            got.append(lax.ppermute(part.astype(BF16), "group", pairs))
    return pl.pallas_call(
        last_kernel,
        out_shape=jax.ShapeDtypeStruct((1, share, width), BF16),
        in_specs=[SMEM, VMEM] + [VMEM] * len(got),
        out_specs=VMEM,
        compiler_params=PARAMS,
        name="last",
    )(sector_sizes, kept, *got)


def solution(mesh):
    return jax.shard_map(
        shards,
        mesh=mesh,
        in_specs=(
            P("sector", None, None),
            P("group", None, None),
            P("group", None, None),
            P(("group", "sector"), None),
            P(("group", "sector")),
            P(),
        ),
        out_specs=P("sector", "group", None),
        check_vma=False,
    )
```

```python
import functools

import jax
import jax.numpy as jnp
from jax import lax
from jax.experimental import pallas as pl
from jax.experimental.pallas import tpu as pltpu
from jax.sharding import PartitionSpec as P

F32 = jnp.float32
BF16 = jnp.bfloat16
VMEM = pl.BlockSpec(memory_space=pltpu.VMEM)
SMEM = pl.BlockSpec(memory_space=pltpu.SMEM)
PARAMS = pltpu.CompilerParams(vmem_limit_bytes=16 * 1024 * 1024)


def dot(a, b, ca, cb):
    return lax.dot_general(a, b, (((ca,), (cb,)), ((), ())), preferred_element_type=F32)


def forward(acc, left, source, right):
    middle = dot(left[...], source[...], 1, 0).astype(BF16)
    acc[...] += dot(middle, right[...], 1, 0)


def adjoint(acc, left, source, right):
    middle = dot(left[...], source[...], 0, 0).astype(BF16)
    acc[...] += dot(middle, right[...], 1, 1)


def friend_of(sector):
    return sector + 1 - 2 * (sector % 2)


def other_of(sector):
    return sector - 1 + 2 * (sector % 2)


def masked(block, size):
    rows = lax.broadcasted_iota(jnp.int32, block.shape, 0)
    cols = lax.broadcasted_iota(jnp.int32, block.shape, 1)
    return jnp.where((rows < size) & (cols < size), block, jnp.zeros_like(block))


def live_terms(codes, owner, want, action):
    for k in range(codes.shape[0]):
        @pl.when(owner + codes[k, 0] - 2 == want)
        def _():
            action(codes[k, 1] - 1, codes[k, 2] - 1)


def codes_kernel(term_list, term_counts, codes):
    for k in range(codes.shape[0]):
        for j in range(codes.shape[1]):
            codes[k, j] = jnp.where(k < term_counts[0], term_list[k, j] + 1, 0)


def near_kernel(own_codes, friend_codes, sizes, own_block, friend_block, left, right, acc, clean, friend_clean):
    here = lax.axis_index("sector")
    friend = friend_of(here)
    clean[...] = masked(own_block[0], sizes[here])
    friend_clean[...] = masked(friend_block[0], sizes[jnp.minimum(friend, sizes.shape[0] - 1)])
    acc[...] = jnp.zeros_like(acc)

    def self_term(l, r):
        forward(acc, left.at[l], clean, right.at[r])
        adjoint(acc, left.at[l], clean, right.at[r])

    live_terms(own_codes, here, here, self_term)
    live_terms(own_codes, here, friend, lambda l, r: adjoint(acc, left.at[l], friend_clean, right.at[r]))
    live_terms(friend_codes, friend, here, lambda l, r: forward(acc, left.at[l], friend_clean, right.at[r]))


def far_kernel(mine, own_codes, other_codes, sizes, other_block, left, right, near, out, clean, acc):
    here = lax.axis_index("sector")
    other = other_of(here)
    share = out.shape[0]
    clean[...] = masked(other_block[0], sizes[jnp.clip(other, 0, sizes.shape[0] - 1)])

    def run(rows):
        acc[...] = near[rows, :]
        live_terms(own_codes, here, other,
                   lambda l, r: adjoint(acc, left.at[l, :, rows], clean, right.at[r]))
        live_terms(other_codes, other, here,
                   lambda l, r: forward(acc, left.at[l, rows, :], clean, right.at[r]))
        out[...] = acc[...].astype(out.dtype)

    if share == near.shape[0]:
        run(slice(None))
        return
    for g in range(near.shape[0] // share):
        @pl.when((lax.axis_index("group") == g) == mine)
        def _():
            run(slice(g * share, (g + 1) * share))


def last_kernel(sizes, kept, *refs):
    got, out = refs[:-1], refs[-1]
    share = kept.shape[0]
    total = kept[...]
    for part in got:
        total = total + part[...].astype(F32)
    rows = lax.broadcasted_iota(jnp.int32, total.shape, 0) + lax.axis_index("group") * share
    cols = lax.broadcasted_iota(jnp.int32, total.shape, 1)
    size = sizes[lax.axis_index("sector")]
    out[0] = jnp.where((rows < size) & (cols < size), total, 0.0).astype(BF16)


def shards(wavefunction, left_factors, right_factors, term_list, term_counts, sector_sizes):
    width = wavefunction.shape[1]
    groups = lax.axis_size("group")
    sectors = lax.axis_size("sector")
    share = width // groups
    friends = [(s, friend_of(s)) for s in range(sectors) if friend_of(s) < sectors]
    others = [(s, other_of(s)) for s in range(sectors) if 0 <= other_of(s) < sectors]
    block = pltpu.VMEM((width, width), BF16)

    hbm = functools.partial(pltpu.with_memory_space_constraint, memory_space=pltpu.HBM)
    other_block = lax.ppermute(wavefunction, "sector", others)
    friend_block = lax.ppermute(wavefunction, "sector", friends)
    codes = pl.pallas_call(
        codes_kernel,
        out_shape=jax.ShapeDtypeStruct(term_list.shape, jnp.int32),
        in_specs=[SMEM, SMEM],
        out_specs=SMEM,
        compiler_params=pltpu.CompilerParams(vmem_limit_bytes=2**20),
        cost_estimate=pl.CostEstimate(flops=10**9, transcendentals=0, bytes_accessed=4 * 2**20),
        name="codes",
    )(hbm(term_list), term_counts)
    friend_codes = lax.ppermute(codes, "sector", friends)
    other_codes = lax.ppermute(codes, "sector", others)
    near = pl.pallas_call(
        near_kernel,
        out_shape=jax.ShapeDtypeStruct((width, width), F32),
        in_specs=[SMEM, SMEM, SMEM, VMEM, VMEM, VMEM, VMEM],
        out_specs=VMEM,
        scratch_shapes=[block, block],
        compiler_params=PARAMS,
        name="near",
    )(codes, friend_codes, sector_sizes, wavefunction, friend_block, left_factors, right_factors)

    def far(rows, mine, dtype):
        return pl.pallas_call(
            functools.partial(far_kernel, mine),
            out_shape=jax.ShapeDtypeStruct((rows, width), dtype),
            in_specs=[SMEM, SMEM, SMEM, VMEM, VMEM, VMEM, VMEM],
            out_specs=VMEM,
            scratch_shapes=[block, pltpu.VMEM((rows, width), F32)],
            compiler_params=PARAMS,
            name="far_mine" if mine else "far_theirs",
        )(codes, other_codes, sector_sizes, other_block, left_factors, right_factors, near)

    hops = [[(g, (g + hop) % groups) for g in range(groups)] for hop in range(1, groups)]
    if groups == 2 and share % 128 == 0:
        theirs = far(share, False, BF16)
        got = [lax.ppermute(theirs, "group", hops[0])]
        kept = far(share, True, F32)
    else:
        whole = far(width, True, F32)
        group = lax.axis_index("group")
        kept = lax.dynamic_slice_in_dim(whole, group * share, share, 0)
        got = []
        for hop, pairs in enumerate(hops, 1):
            part = lax.dynamic_slice_in_dim(whole, (group + hop) % groups * share, share, 0)
            got.append(lax.ppermute(part.astype(BF16), "group", pairs))
    return pl.pallas_call(
        last_kernel,
        out_shape=jax.ShapeDtypeStruct((1, share, width), BF16),
        in_specs=[SMEM, VMEM] + [VMEM] * len(got),
        out_specs=VMEM,
        compiler_params=PARAMS,
        name="last",
    )(sector_sizes, kept, *got)


def solution(mesh):
    return jax.shard_map(
        shards,
        mesh=mesh,
        in_specs=(
            P("sector", None, None),
            P("group", None, None),
            P("group", None, None),
            P(("group", "sector"), None),
            P(("group", "sector")),
            P(),
        ),
        out_specs=P("sector", "group", None),
        check_vma=False,
    )
```

```python
import functools

import jax
import jax.numpy as jnp
from jax import lax
from jax.experimental import pallas as pl
from jax.experimental.pallas import tpu as pltpu
from jax.sharding import PartitionSpec as P

F32 = jnp.float32
BF16 = jnp.bfloat16
VMEM = pl.BlockSpec(memory_space=pltpu.VMEM)
SMEM = pl.BlockSpec(memory_space=pltpu.SMEM)
PARAMS = pltpu.CompilerParams(vmem_limit_bytes=16 * 1024 * 1024)


def dot(a, b, ca, cb):
    return lax.dot_general(a, b, (((ca,), (cb,)), ((), ())), preferred_element_type=F32)


def forward(acc, left, source, right):
    middle = dot(left[...], source[...], 1, 0).astype(BF16)
    acc[...] += dot(middle, right[...], 1, 0)


def adjoint(acc, left, source, right):
    middle = dot(left[...], source[...], 0, 0).astype(BF16)
    acc[...] += dot(middle, right[...], 1, 1)


def friend_of(sector):
    return sector + 1 - 2 * (sector % 2)


def other_of(sector):
    return sector - 1 + 2 * (sector % 2)


def masked(block, size, first=0):
    rows = lax.broadcasted_iota(jnp.int32, block.shape, 0) + first
    cols = lax.broadcasted_iota(jnp.int32, block.shape, 1)
    return jnp.where((rows < size) & (cols < size), block, jnp.zeros_like(block))


def live_terms(codes, owner, want, action):
    for k in range(codes.shape[0]):
        @pl.when(owner + codes[k, 0] - 2 == want)
        def _():
            action(codes[k, 1] - 1, codes[k, 2] - 1)


def codes_kernel(term_list, term_counts, codes):
    slot = lax.broadcasted_iota(jnp.int32, codes.shape, 0)
    codes[...] = jnp.where(slot < term_counts[...], term_list[...] + 1, 0)


def near_kernel(own_codes, friend_codes, sizes, own_block, friend_block, left, right, acc, clean, friend_clean):
    here = lax.axis_index("sector")
    friend = friend_of(here)
    clean[...] = masked(own_block[0], sizes[here])
    friend_clean[...] = masked(friend_block[0], sizes[jnp.minimum(friend, sizes.shape[0] - 1)])
    acc[...] = jnp.zeros_like(acc)

    def self_term(l, r):
        forward(acc, left.at[l], clean, right.at[r])
        adjoint(acc, left.at[l], clean, right.at[r])

    live_terms(own_codes, here, here, self_term)
    live_terms(own_codes, here, friend, lambda l, r: adjoint(acc, left.at[l], friend_clean, right.at[r]))
    live_terms(friend_codes, friend, here, lambda l, r: forward(acc, left.at[l], friend_clean, right.at[r]))


def far_kernel(mine, own_codes, other_codes, sizes, other_block, left, right, near, out, clean, acc):
    here = lax.axis_index("sector")
    other = other_of(here)
    share = out.shape[0]
    clean[...] = masked(other_block[0], sizes[jnp.clip(other, 0, sizes.shape[0] - 1)])

    def run(rows):
        first = rows.start or 0
        acc[...] = near[rows, :]
        live_terms(own_codes, here, other,
                   lambda l, r: adjoint(acc, left.at[l, :, rows], clean, right.at[r]))
        live_terms(other_codes, other, here,
                   lambda l, r: forward(acc, left.at[l, rows, :], clean, right.at[r]))
        out[...] = masked(acc[...], sizes[here], first).astype(out.dtype)

    if share == near.shape[0]:
        run(slice(None))
        return
    for g in range(near.shape[0] // share):
        @pl.when((lax.axis_index("group") == g) == mine)
        def _():
            run(slice(g * share, (g + 1) * share))


def last_kernel(kept, *refs):
    total = kept[...]
    for part in refs[:-1]:
        total = total + part[...].astype(F32)
    refs[-1][0] = total.astype(BF16)


def shards(wavefunction, left_factors, right_factors, term_list, term_counts, sector_sizes):
    width = wavefunction.shape[1]
    groups = lax.axis_size("group")
    sectors = lax.axis_size("sector")
    share = width // groups
    friends = [(s, friend_of(s)) for s in range(sectors) if friend_of(s) < sectors]
    others = [(s, other_of(s)) for s in range(sectors) if 0 <= other_of(s) < sectors]
    block = pltpu.VMEM((width, width), BF16)

    hbm = functools.partial(pltpu.with_memory_space_constraint, memory_space=pltpu.HBM)
    other_block = lax.ppermute(wavefunction, "sector", others)
    friend_block = lax.ppermute(wavefunction, "sector", friends)
    codes = pl.pallas_call(
        codes_kernel,
        out_shape=jax.ShapeDtypeStruct(term_list.shape, jnp.int32),
        in_specs=[VMEM, VMEM],
        out_specs=VMEM,
        compiler_params=pltpu.CompilerParams(vmem_limit_bytes=2**20),
        cost_estimate=pl.CostEstimate(flops=10**9, transcendentals=0, bytes_accessed=4 * 2**20),
        name="codes",
    )(hbm(term_list), term_counts[:, None])
    friend_codes = lax.ppermute(codes, "sector", friends)
    other_codes = lax.ppermute(codes, "sector", others)
    near = pl.pallas_call(
        near_kernel,
        out_shape=jax.ShapeDtypeStruct((width, width), F32),
        in_specs=[SMEM, SMEM, SMEM, VMEM, VMEM, VMEM, VMEM],
        out_specs=VMEM,
        scratch_shapes=[block, block],
        compiler_params=PARAMS,
        name="near",
    )(codes, friend_codes, sector_sizes, wavefunction, friend_block, left_factors, right_factors)

    def far(rows, mine, dtype):
        return pl.pallas_call(
            functools.partial(far_kernel, mine),
            out_shape=jax.ShapeDtypeStruct((rows, width), dtype),
            in_specs=[SMEM, SMEM, SMEM, VMEM, VMEM, VMEM, VMEM],
            out_specs=VMEM,
            scratch_shapes=[block, pltpu.VMEM((rows, width), F32)],
            compiler_params=PARAMS,
            name="far_mine" if mine else "far_theirs",
        )(codes, other_codes, sector_sizes, other_block, left_factors, right_factors, near)

    hops = [[(g, (g + hop) % groups) for g in range(groups)] for hop in range(1, groups)]
    if groups == 2 and share % 128 == 0:
        theirs = far(share, False, BF16)
        got = [lax.ppermute(theirs, "group", hops[0])]
        kept = far(share, True, F32)
    else:
        whole = far(width, True, F32)
        group = lax.axis_index("group")
        kept = lax.dynamic_slice_in_dim(whole, group * share, share, 0)
        got = []
        for hop, pairs in enumerate(hops, 1):
            part = lax.dynamic_slice_in_dim(whole, (group + hop) % groups * share, share, 0)
            got.append(lax.ppermute(part.astype(BF16), "group", pairs))
    return pl.pallas_call(
        last_kernel,
        out_shape=jax.ShapeDtypeStruct((1, share, width), BF16),
        in_specs=[VMEM] * (1 + len(got)),
        out_specs=VMEM,
        compiler_params=PARAMS,
        name="last",
    )(kept, *got)


def solution(mesh):
    return jax.shard_map(
        shards,
        mesh=mesh,
        in_specs=(
            P("sector", None, None),
            P("group", None, None),
            P("group", None, None),
            P(("group", "sector"), None),
            P(("group", "sector")),
            P(),
        ),
        out_specs=P("sector", "group", None),
        check_vma=False,
    )
```

```python
import functools

import jax
import jax.numpy as jnp
from jax import lax
from jax.experimental import pallas as pl
from jax.experimental.pallas import tpu as pltpu
from jax.sharding import PartitionSpec as P

F32 = jnp.float32
BF16 = jnp.bfloat16
VMEM = pl.BlockSpec(memory_space=pltpu.VMEM)
SMEM = pl.BlockSpec(memory_space=pltpu.SMEM)
PARAMS = pltpu.CompilerParams(vmem_limit_bytes=24 * 1024 * 1024)


def dot(a, b, ca, cb):
    return lax.dot_general(a, b, (((ca,), (cb,)), ((), ())), preferred_element_type=F32)


def forward(acc, left, source, right):
    middle = dot(left[...], source[...], 1, 0).astype(BF16)
    acc[...] += dot(middle, right[...], 1, 0)


def adjoint(acc, left, source, right):
    middle = dot(left[...], source[...], 0, 0).astype(BF16)
    acc[...] += dot(middle, right[...], 1, 1)


def friend_of(sector):
    return sector + 1 - 2 * (sector % 2)


def other_of(sector):
    return sector - 1 + 2 * (sector % 2)


def masked(block, size, first=0):
    rows = lax.broadcasted_iota(jnp.int32, block.shape, 0) + first
    cols = lax.broadcasted_iota(jnp.int32, block.shape, 1)
    return jnp.where((rows < size) & (cols < size), block, jnp.zeros_like(block))


def live_terms(codes, owner, want, action):
    for k in range(codes.shape[0]):
        @pl.when(owner + codes[k, 0] - 2 == want)
        def _():
            action(codes[k, 1] - 1, codes[k, 2] - 1)


def codes_kernel(term_list, term_counts, codes):
    slot = lax.broadcasted_iota(jnp.int32, codes.shape, 0)
    codes[...] = jnp.where(slot < term_counts[...], term_list[...] + 1, 0)


def near_kernel(own_codes, friend_codes, sizes, own_block, friend_block, left, right, acc, clean, friend_clean):
    here = lax.axis_index("sector")
    friend = friend_of(here)
    clean[...] = masked(own_block[0], sizes[here])
    friend_clean[...] = masked(friend_block[0], sizes[jnp.minimum(friend, sizes.shape[0] - 1)])
    acc[...] = jnp.zeros_like(acc)

    def self_term(l, r):
        forward(acc, left.at[l], clean, right.at[r])
        adjoint(acc, left.at[l], clean, right.at[r])

    live_terms(own_codes, here, here, self_term)
    live_terms(own_codes, here, friend, lambda l, r: adjoint(acc, left.at[l], friend_clean, right.at[r]))
    live_terms(friend_codes, friend, here, lambda l, r: forward(acc, left.at[l], friend_clean, right.at[r]))


def prep_kernel(own_codes, other_codes, sizes, left, right, plan, lhs, rhs, count):
    here = lax.axis_index("sector")
    other = other_of(here)
    size = sizes[jnp.clip(other, 0, sizes.shape[0] - 1)]
    shape = lhs.shape[1:]
    inside_cols = lax.broadcasted_iota(jnp.int32, shape, 1) < size
    inside_rows = lax.broadcasted_iota(jnp.int32, shape, 0) < size
    count[0] = 0

    def add(a, b):
        i = count[0]
        lhs[i] = jnp.where(inside_cols, a, jnp.zeros_like(a))
        rhs[i] = jnp.where(inside_rows, b, jnp.zeros_like(b))
        count[0] = i + 1

    live_terms(own_codes, here, other, lambda l, r: add(left[l].T, right[r].T))
    live_terms(other_codes, other, here, lambda l, r: add(left[l], right[r]))
    plan[...] = jnp.where(lax.broadcasted_iota(jnp.int32, plan.shape, 1) == 0, count[0], sizes[here])


def far_kernel(groups, hops, plan, block, lhs, rhs, near, out, acc):
    share, width = acc.shape
    live, size = plan[0, 0], plan[0, 1]

    def terms(i, n, rows):
        a = lhs[pl.ds(i, n), rows, :].reshape(n * share, width)
        middle = dot(a, block[0], 1, 0).astype(BF16)
        middle = jnp.concatenate([middle[j * share:(j + 1) * share] for j in range(n)], axis=1)
        acc[...] += dot(middle, rhs[pl.ds(i, n)].reshape(n * width, width), 1, 0)

    for j, hop in enumerate(hops):
        first = pl.multiple_of((lax.axis_index("group") + hop) % groups * share, share)
        rows = pl.ds(first, share)
        acc[...] = near[rows, :]

        def pair(i, carry):
            terms(2 * i, 2, rows)
            return carry

        lax.fori_loop(0, live // 2, pair, 0)

        @pl.when(live % 2 == 1)
        def _():
            terms(live - 1, 1, rows)

        out[j] = masked(acc[...], size, first).astype(out.dtype)


def last_kernel(kept, *refs):
    total = kept[0]
    for part in refs[:-1]:
        total = total + part[0].astype(F32)
    refs[-1][0] = total.astype(BF16)


def shards(wavefunction, left_factors, right_factors, term_list, term_counts, sector_sizes):
    width = wavefunction.shape[1]
    groups = lax.axis_size("group")
    sectors = lax.axis_size("sector")
    share = width // groups
    friends = [(s, friend_of(s)) for s in range(sectors) if friend_of(s) < sectors]
    others = [(s, other_of(s)) for s in range(sectors) if 0 <= other_of(s) < sectors]
    block = pltpu.VMEM((width, width), BF16)

    hbm = functools.partial(pltpu.with_memory_space_constraint, memory_space=pltpu.HBM)
    other_block = lax.ppermute(wavefunction, "sector", others)
    friend_block = lax.ppermute(wavefunction, "sector", friends)
    codes = pl.pallas_call(
        codes_kernel,
        out_shape=jax.ShapeDtypeStruct(term_list.shape, jnp.int32),
        in_specs=[VMEM, VMEM],
        out_specs=VMEM,
        compiler_params=pltpu.CompilerParams(vmem_limit_bytes=2**20),
        cost_estimate=pl.CostEstimate(flops=4 * 10**9, transcendentals=0, bytes_accessed=4 * 2**22),
        name="codes",
    )(hbm(term_list), term_counts[:, None])
    friend_codes = lax.ppermute(codes, "sector", friends)
    other_codes = lax.ppermute(codes, "sector", others)
    near = pl.pallas_call(
        near_kernel,
        out_shape=jax.ShapeDtypeStruct((width, width), F32),
        in_specs=[SMEM, SMEM, SMEM, VMEM, VMEM, VMEM, VMEM],
        out_specs=VMEM,
        scratch_shapes=[block, block],
        compiler_params=PARAMS,
        name="near",
    )(codes, friend_codes, sector_sizes, wavefunction, friend_block, left_factors, right_factors)

    terms = 2 * term_list.shape[0]
    plan, lhs, rhs = pl.pallas_call(
        prep_kernel,
        out_shape=[
            jax.ShapeDtypeStruct((1, 2), jnp.int32),
            jax.ShapeDtypeStruct((terms, width, width), BF16),
            jax.ShapeDtypeStruct((terms, width, width), BF16),
        ],
        in_specs=[SMEM, SMEM, SMEM, VMEM, VMEM],
        out_specs=[VMEM, VMEM, VMEM],
        scratch_shapes=[pltpu.SMEM((1,), jnp.int32)],
        compiler_params=PARAMS,
        name="prep",
    )(codes, other_codes, sector_sizes, left_factors, right_factors)

    def far(hops, dtype):
        return pl.pallas_call(
            functools.partial(far_kernel, groups, hops),
            out_shape=jax.ShapeDtypeStruct((len(hops), share, width), dtype),
            in_specs=[SMEM, VMEM, VMEM, VMEM, VMEM],
            out_specs=VMEM,
            scratch_shapes=[pltpu.VMEM((share, width), F32)],
            compiler_params=PARAMS,
        )(plan, other_block, lhs, rhs, near)

    hops = range(1, groups)
    got = []
    if groups > 1:
        theirs = far(hops, BF16)
        for j, hop in enumerate(hops):
            got.append(lax.ppermute(theirs[j:j + 1], "group", [(g, (g + hop) % groups) for g in range(groups)]))
    kept = far((0,), F32)
    return pl.pallas_call(
        last_kernel,
        out_shape=jax.ShapeDtypeStruct((1, share, width), BF16),
        in_specs=[VMEM] * (1 + len(got)),
        out_specs=VMEM,
        compiler_params=PARAMS,
        name="last",
    )(kept, *got)


def solution(mesh):
    return jax.shard_map(
        shards,
        mesh=mesh,
        in_specs=(
            P("sector", None, None),
            P("group", None, None),
            P("group", None, None),
            P(("group", "sector"), None),
            P(("group", "sector")),
            P(),
        ),
        out_specs=P("sector", "group", None),
        check_vma=False,
    )
```

```python
import functools

import jax
import jax.numpy as jnp
from jax import lax
from jax.experimental import pallas as pl
from jax.experimental.pallas import tpu as pltpu
from jax.sharding import PartitionSpec as P

F32 = jnp.float32
BF16 = jnp.bfloat16
VMEM = pl.BlockSpec(memory_space=pltpu.VMEM)
SMEM = pl.BlockSpec(memory_space=pltpu.SMEM)
PARAMS = pltpu.CompilerParams(vmem_limit_bytes=24 * 1024 * 1024)


def dot(a, b, ca, cb):
    return lax.dot_general(a, b, (((ca,), (cb,)), ((), ())), preferred_element_type=F32)


def forward(acc, left, source, right):
    middle = dot(left[...], source[...], 1, 0).astype(BF16)
    acc[...] += dot(middle, right[...], 1, 0)


def adjoint(acc, left, source, right):
    middle = dot(left[...], source[...], 0, 0).astype(BF16)
    acc[...] += dot(middle, right[...], 1, 1)


def friend_of(sector):
    return sector + 1 - 2 * (sector % 2)


def other_of(sector):
    return sector - 1 + 2 * (sector % 2)


def masked(block, size, first=0):
    rows = lax.broadcasted_iota(jnp.int32, block.shape, 0) + first
    cols = lax.broadcasted_iota(jnp.int32, block.shape, 1)
    return jnp.where((rows < size) & (cols < size), block, jnp.zeros_like(block))


def live_terms(codes, owner, want, action):
    for k in range(codes.shape[0]):
        @pl.when(owner + codes[k, 0] - 2 == want)
        def _():
            action(codes[k, 1] - 1, codes[k, 2] - 1)


def codes_kernel(term_list, term_counts, codes):
    slot = lax.broadcasted_iota(jnp.int32, codes.shape, 0)
    codes[...] = jnp.where(slot < term_counts[...], term_list[...] + 1, 0)


def near_kernel(own_codes, friend_codes, sizes, own_block, friend_block, left, right, acc, clean, friend_clean):
    here = lax.axis_index("sector")
    friend = friend_of(here)
    clean[...] = masked(own_block[0], sizes[here])
    friend_clean[...] = masked(friend_block[0], sizes[jnp.minimum(friend, sizes.shape[0] - 1)])
    acc[...] = jnp.zeros_like(acc)

    def self_term(l, r):
        forward(acc, left.at[l], clean, right.at[r])
        adjoint(acc, left.at[l], clean, right.at[r])

    live_terms(own_codes, here, here, self_term)
    live_terms(own_codes, here, friend, lambda l, r: adjoint(acc, left.at[l], friend_clean, right.at[r]))
    live_terms(friend_codes, friend, here, lambda l, r: forward(acc, left.at[l], friend_clean, right.at[r]))


def prep_kernel(sizes, left, right, lhs, rhs):
    other = other_of(lax.axis_index("sector"))
    size = sizes[jnp.clip(other, 0, sizes.shape[0] - 1)]
    count, *shape = left.shape
    inside_cols = lax.broadcasted_iota(jnp.int32, shape, 1) < size
    inside_rows = lax.broadcasted_iota(jnp.int32, shape, 0) < size

    def one(i, carry):
        a, b = left[i], right[i]
        lhs[i] = jnp.where(inside_cols, a, jnp.zeros_like(a))
        rhs[i] = jnp.where(inside_rows, b, jnp.zeros_like(b))
        lhs[count + i] = jnp.where(inside_cols, a.T, jnp.zeros_like(a))
        rhs[count + i] = jnp.where(inside_rows, b.T, jnp.zeros_like(b))
        return carry

    lax.fori_loop(0, count, one, 0)


def far_kernel(groups, hops, own_codes, other_codes, sizes, block, lhs, rhs, near, out, acc, left_picks, right_picks):
    share, _ = acc.shape
    here = lax.axis_index("sector")
    other = other_of(here)
    count = lhs.shape[0] // 2
    live = jnp.int32(0)
    for codes, owner, want, skip in ((own_codes, here, other, count), (other_codes, other, here, 0)):
        for k in range(codes.shape[0]):
            left_picks[live] = skip + codes[k, 1] - 1
            right_picks[live] = skip + codes[k, 2] - 1
            live += (owner + codes[k, 0] - 2 == want).astype(jnp.int32)

    def terms(i, n, rows):
        a = jnp.concatenate([lhs[left_picks[i + j], rows, :] for j in range(n)], axis=0)
        b = jnp.concatenate([rhs[right_picks[i + j]] for j in range(n)], axis=0)
        middle = dot(a, block[0], 1, 0).astype(BF16)
        middle = jnp.concatenate([middle[j * share:(j + 1) * share] for j in range(n)], axis=1)
        acc[...] += dot(middle, b, 1, 0)

    for j, hop in enumerate(hops):
        first = pl.multiple_of((lax.axis_index("group") + hop) % groups * share, share)
        rows = pl.ds(first, share)
        acc[...] = near[rows, :]

        def pair(i, carry):
            terms(2 * i, 2, rows)
            return carry

        lax.fori_loop(0, live // 2, pair, 0)

        @pl.when(live % 2 == 1)
        def _():
            terms(live - 1, 1, rows)

        out[j] = masked(acc[...], sizes[here], first).astype(out.dtype)


def last_kernel(kept, *refs):
    total = kept[0]
    for part in refs[:-1]:
        total = total + part[0].astype(F32)
    refs[-1][0] = total.astype(BF16)


def shards(wavefunction, left_factors, right_factors, term_list, term_counts, sector_sizes):
    width = wavefunction.shape[1]
    groups = lax.axis_size("group")
    sectors = lax.axis_size("sector")
    share = width // groups
    friends = [(s, friend_of(s)) for s in range(sectors) if friend_of(s) < sectors]
    others = [(s, other_of(s)) for s in range(sectors) if 0 <= other_of(s) < sectors]
    block = pltpu.VMEM((width, width), BF16)

    hbm = functools.partial(pltpu.with_memory_space_constraint, memory_space=pltpu.HBM)
    other_block = lax.ppermute(wavefunction, "sector", others)
    friend_block = lax.ppermute(wavefunction, "sector", friends)
    codes = pl.pallas_call(
        codes_kernel,
        out_shape=jax.ShapeDtypeStruct(term_list.shape, jnp.int32),
        in_specs=[VMEM, VMEM],
        out_specs=VMEM,
        compiler_params=pltpu.CompilerParams(vmem_limit_bytes=2**20),
        cost_estimate=pl.CostEstimate(flops=4 * 10**9, transcendentals=0, bytes_accessed=4 * 2**22),
        name="codes",
    )(hbm(term_list), term_counts[:, None])
    friend_codes = lax.ppermute(codes, "sector", friends)
    other_codes = lax.ppermute(codes, "sector", others)
    near = pl.pallas_call(
        near_kernel,
        out_shape=jax.ShapeDtypeStruct((width, width), F32),
        in_specs=[SMEM, SMEM, SMEM, VMEM, VMEM, VMEM, VMEM],
        out_specs=VMEM,
        scratch_shapes=[block, block],
        compiler_params=PARAMS,
        name="near",
    )(codes, friend_codes, sector_sizes, wavefunction, friend_block, left_factors, right_factors)

    laid_out = jax.ShapeDtypeStruct((2 * left_factors.shape[0], width, width), BF16)
    lhs, rhs = pl.pallas_call(
        prep_kernel,
        out_shape=[laid_out, laid_out],
        in_specs=[SMEM, VMEM, VMEM],
        out_specs=[VMEM, VMEM],
        compiler_params=PARAMS,
        name="prep",
    )(sector_sizes, left_factors, right_factors)
    picks = pltpu.SMEM((2 * term_list.shape[0],), jnp.int32)

    def far(hops, dtype):
        return pl.pallas_call(
            functools.partial(far_kernel, groups, hops),
            out_shape=jax.ShapeDtypeStruct((len(hops), share, width), dtype),
            in_specs=[SMEM, SMEM, SMEM, VMEM, VMEM, VMEM, VMEM],
            out_specs=VMEM,
            scratch_shapes=[pltpu.VMEM((share, width), F32), picks, picks],
            compiler_params=PARAMS,
        )(codes, other_codes, sector_sizes, other_block, lhs, rhs, near)

    hops = range(1, groups)
    got = []
    if groups > 1:
        theirs = far(hops, BF16)
        for j, hop in enumerate(hops):
            got.append(lax.ppermute(theirs[j:j + 1], "group", [(g, (g + hop) % groups) for g in range(groups)]))
    kept = far((0,), F32)
    return pl.pallas_call(
        last_kernel,
        out_shape=jax.ShapeDtypeStruct((1, share, width), BF16),
        in_specs=[VMEM] * (1 + len(got)),
        out_specs=VMEM,
        compiler_params=PARAMS,
        name="last",
    )(kept, *got)


def solution(mesh):
    return jax.shard_map(
        shards,
        mesh=mesh,
        in_specs=(
            P("sector", None, None),
            P("group", None, None),
            P("group", None, None),
            P(("group", "sector"), None),
            P(("group", "sector")),
            P(),
        ),
        out_specs=P("sector", "group", None),
        check_vma=False,
    )
```

```python
import functools

import jax
import jax.numpy as jnp
from jax import lax
from jax.experimental import pallas as pl
from jax.experimental.pallas import tpu as pltpu
from jax.sharding import PartitionSpec as P

F32 = jnp.float32
BF16 = jnp.bfloat16
VMEM = pl.BlockSpec(memory_space=pltpu.VMEM)
SMEM = pl.BlockSpec(memory_space=pltpu.SMEM)
PARAMS = pltpu.CompilerParams(vmem_limit_bytes=16 * 1024 * 1024)


def dot(a, b, ca, cb):
    return lax.dot_general(a, b, (((ca,), (cb,)), ((), ())), preferred_element_type=F32)


def forward(acc, left, source, right):
    middle = dot(left[...], source[...], 1, 0).astype(BF16)
    acc[...] += dot(middle, right[...], 1, 0)


def adjoint(acc, left, source, right):
    middle = dot(left[...], source[...], 0, 0).astype(BF16)
    acc[...] += dot(middle, right[...], 1, 1)


def friend_of(sector):
    return sector + 1 - 2 * (sector % 2)


def other_of(sector):
    return sector - 1 + 2 * (sector % 2)


def masked(block, size, first=0):
    rows = lax.broadcasted_iota(jnp.int32, block.shape, 0) + first
    cols = lax.broadcasted_iota(jnp.int32, block.shape, 1)
    return jnp.where((rows < size) & (cols < size), block, jnp.zeros_like(block))


def cleaned(block, size):
    rows = lax.broadcasted_iota(jnp.int32, (block.shape[0], 1), 0) < size
    cols = lax.broadcasted_iota(jnp.int32, (1, block.shape[1]), 1) < size
    return block * rows.astype(BF16) * cols.astype(BF16)


def live_terms(codes, owner, want, action):
    for k in range(codes.shape[0]):
        @pl.when(owner + codes[k, 0] - 2 == want)
        def _():
            action(codes[k, 1] - 1, codes[k, 2] - 1)


def codes_kernel(term_list, term_counts, codes):
    slot = lax.broadcasted_iota(jnp.int32, codes.shape, 0)
    codes[...] = jnp.where(slot < term_counts[...], term_list[...] + 1, 0)


def near_kernel(own_codes, friend_codes, sizes, own_block, friend_block, left, right, acc, clean, friend_clean):
    here = lax.axis_index("sector")
    friend = friend_of(here)
    clean[...] = cleaned(own_block[0], sizes[here])
    friend_clean[...] = cleaned(friend_block[0], sizes[jnp.minimum(friend, sizes.shape[0] - 1)])
    acc[...] = jnp.zeros_like(acc)

    def self_term(l, r):
        forward(acc, left.at[l], clean, right.at[r])
        adjoint(acc, left.at[l], clean, right.at[r])

    live_terms(own_codes, here, here, self_term)
    live_terms(own_codes, here, friend, lambda l, r: adjoint(acc, left.at[l], friend_clean, right.at[r]))
    live_terms(friend_codes, friend, here, lambda l, r: forward(acc, left.at[l], friend_clean, right.at[r]))


def picked(codes, owner, want, lefts, rights):
    live = jnp.int32(0)
    for k in range(codes.shape[0]):
        lefts[live] = codes[k, 1] - 1
        rights[live] = codes[k, 2] - 1
        live += (owner + codes[k, 0] - 2 == want).astype(jnp.int32)
    return live


def in_pairs(live, terms):
    def pair(i, carry):
        terms(2 * i, 2)
        return carry

    lax.fori_loop(0, live // 2, pair, 0)

    @pl.when(live % 2 == 1)
    def _():
        terms(live - 1, 1)


def side_by_side(stacked, n):
    rows = stacked.shape[0] // n
    return jnp.concatenate([stacked[j * rows:(j + 1) * rows] for j in range(n)], axis=1)


def far_kernel(mine, own_codes, other_codes, sizes, other_block, left, right, near, out, clean, acc,
               own_left, own_right, other_left, other_right):
    here = lax.axis_index("sector")
    other = other_of(here)
    share = out.shape[0]
    clean[...] = cleaned(other_block[0], sizes[jnp.clip(other, 0, sizes.shape[0] - 1)])
    adjoints = picked(own_codes, here, other, own_left, own_right)
    forwards = picked(other_codes, other, here, other_left, other_right)

    def run(rows):
        first = rows.start or 0
        acc[...] = near[rows, :]

        def forward_terms(i, n):
            lefts = jnp.concatenate([left[other_left[i + j], rows, :] for j in range(n)], axis=0)
            rights = jnp.concatenate([right[other_right[i + j]] for j in range(n)], axis=0)
            middle = dot(lefts, clean[...], 1, 0).astype(BF16)
            acc[...] += dot(side_by_side(middle, n), rights, 1, 0)

        def adjoint_terms(i, n):
            lefts = jnp.concatenate([left[own_left[i + j], :, rows] for j in range(n)], axis=1)
            rights = jnp.concatenate([right[own_right[i + j]] for j in range(n)], axis=1)
            middle = dot(lefts, clean[...], 0, 0).astype(BF16)
            acc[...] += dot(side_by_side(middle, n), rights, 1, 1)

        in_pairs(forwards, forward_terms)
        in_pairs(adjoints, adjoint_terms)
        out[...] = masked(acc[...], sizes[here], first).astype(out.dtype)

    if share == near.shape[0]:
        run(slice(None))
        return
    for g in range(near.shape[0] // share):
        @pl.when((lax.axis_index("group") == g) == mine)
        def _():
            run(slice(g * share, (g + 1) * share))


def last_kernel(kept, *refs):
    total = kept[...]
    for part in refs[:-1]:
        total = total + part[...].astype(F32)
    refs[-1][0] = total.astype(BF16)


def shards(wavefunction, left_factors, right_factors, term_list, term_counts, sector_sizes):
    width = wavefunction.shape[1]
    groups = lax.axis_size("group")
    sectors = lax.axis_size("sector")
    share = width // groups
    friends = [(s, friend_of(s)) for s in range(sectors) if friend_of(s) < sectors]
    others = [(s, other_of(s)) for s in range(sectors) if 0 <= other_of(s) < sectors]
    block = pltpu.VMEM((width, width), BF16)

    hbm = functools.partial(pltpu.with_memory_space_constraint, memory_space=pltpu.HBM)
    other_block = lax.ppermute(wavefunction, "sector", others)
    friend_block = lax.ppermute(wavefunction, "sector", friends)
    codes = pl.pallas_call(
        codes_kernel,
        out_shape=jax.ShapeDtypeStruct(term_list.shape, jnp.int32),
        in_specs=[VMEM, VMEM],
        out_specs=VMEM,
        compiler_params=pltpu.CompilerParams(vmem_limit_bytes=2**20),
        cost_estimate=pl.CostEstimate(flops=4 * 10**9, transcendentals=0, bytes_accessed=2**24),
        name="codes",
    )(hbm(term_list), term_counts[:, None])
    friend_codes = lax.ppermute(codes, "sector", friends)
    other_codes = lax.ppermute(codes, "sector", others)
    near = pl.pallas_call(
        near_kernel,
        out_shape=jax.ShapeDtypeStruct((width, width), F32),
        in_specs=[SMEM, SMEM, SMEM, VMEM, VMEM, VMEM, VMEM],
        out_specs=VMEM,
        scratch_shapes=[block, block],
        compiler_params=PARAMS,
        name="near",
    )(codes, friend_codes, sector_sizes, wavefunction, friend_block, left_factors, right_factors)

    picks = pltpu.SMEM((term_list.shape[0],), jnp.int32)

    def far(rows, mine, dtype):
        return pl.pallas_call(
            functools.partial(far_kernel, mine),
            out_shape=jax.ShapeDtypeStruct((rows, width), dtype),
            in_specs=[SMEM, SMEM, SMEM, VMEM, VMEM, VMEM, VMEM],
            out_specs=VMEM,
            scratch_shapes=[block, pltpu.VMEM((rows, width), F32)] + [picks] * 4,
            compiler_params=PARAMS,
            name="far_mine" if mine else "far_theirs",
        )(codes, other_codes, sector_sizes, other_block, left_factors, right_factors, near)

    hops = [[(g, (g + hop) % groups) for g in range(groups)] for hop in range(1, groups)]
    if groups == 2 and share % 128 == 0:
        theirs = far(share, False, BF16)
        got = [lax.ppermute(theirs, "group", hops[0])]
        kept = far(share, True, F32)
    else:
        whole = far(width, True, F32)
        group = lax.axis_index("group")
        kept = lax.dynamic_slice_in_dim(whole, group * share, share, 0)
        got = []
        for hop, pairs in enumerate(hops, 1):
            part = lax.dynamic_slice_in_dim(whole, (group + hop) % groups * share, share, 0)
            got.append(lax.ppermute(part.astype(BF16), "group", pairs))
    return pl.pallas_call(
        last_kernel,
        out_shape=jax.ShapeDtypeStruct((1, share, width), BF16),
        in_specs=[VMEM] * (1 + len(got)),
        out_specs=VMEM,
        compiler_params=PARAMS,
        name="last",
    )(kept, *got)


def solution(mesh):
    return jax.shard_map(
        shards,
        mesh=mesh,
        in_specs=(
            P("sector", None, None),
            P("group", None, None),
            P("group", None, None),
            P(("group", "sector"), None),
            P(("group", "sector")),
            P(),
        ),
        out_specs=P("sector", "group", None),
        check_vma=False,
    )
```

```python
import functools

import jax
import jax.numpy as jnp
from jax import lax
from jax.experimental import pallas as pl
from jax.experimental.pallas import tpu as pltpu
from jax.sharding import PartitionSpec as P

F32 = jnp.float32
BF16 = jnp.bfloat16
VMEM = pl.BlockSpec(memory_space=pltpu.VMEM)
SMEM = pl.BlockSpec(memory_space=pltpu.SMEM)
PARAMS = pltpu.CompilerParams(vmem_limit_bytes=16 * 1024 * 1024)


def dot(a, b, ca, cb):
    return lax.dot_general(a, b, (((ca,), (cb,)), ((), ())), preferred_element_type=F32)


def forward(acc, left, source, right):
    middle = dot(left[...], source[...], 1, 0).astype(BF16)
    acc[...] += dot(middle, right[...], 1, 0)


def adjoint(acc, left, source, right):
    middle = dot(left[...], source[...], 0, 0).astype(BF16)
    acc[...] += dot(middle, right[...], 1, 1)


def friend_of(sector):
    return sector + 1 - 2 * (sector % 2)


def other_of(sector):
    return sector - 1 + 2 * (sector % 2)


def masked(block, size, first=0):
    rows = lax.broadcasted_iota(jnp.int32, block.shape, 0) + first
    cols = lax.broadcasted_iota(jnp.int32, block.shape, 1)
    return jnp.where((rows < size) & (cols < size), block, jnp.zeros_like(block))


def cleaned(block, size):
    rows = lax.broadcasted_iota(jnp.int32, (block.shape[0], 1), 0) < size
    cols = lax.broadcasted_iota(jnp.int32, (1, block.shape[1]), 1) < size
    return block * rows.astype(BF16) * cols.astype(BF16)


def live_terms(codes, owner, want, action):
    for k in range(codes.shape[0]):
        @pl.when(owner + codes[k, 0] - 2 == want)
        def _():
            action(codes[k, 1] - 1, codes[k, 2] - 1)


def codes_kernel(term_list, term_counts, codes):
    slot = lax.broadcasted_iota(jnp.int32, codes.shape, 0)
    codes[...] = jnp.where(slot < term_counts[...], term_list[...] + 1, 0)


def near_kernel(own_codes, friend_codes, sizes, own_block, friend_block, left, right,
                acc, plan, clean, friend_clean, lefts, rights):
    here = lax.axis_index("sector")
    friend = friend_of(here)
    other = other_of(here)
    slots = own_codes.shape[0]
    adjoints = picked(own_codes, here, other, lefts, rights)
    scalars = [sizes[here], sizes[jnp.clip(other, 0, sizes.shape[0] - 1)], adjoints]
    plan[...] = written(scalars + [lefts[k] for k in range(slots)] + [rights[k] for k in range(slots)])
    clean[...] = cleaned(own_block[0], sizes[here])
    friend_clean[...] = cleaned(friend_block[0], sizes[jnp.minimum(friend, sizes.shape[0] - 1)])
    acc[...] = jnp.zeros_like(acc)

    def self_term(l, r):
        forward(acc, left.at[l], clean, right.at[r])
        adjoint(acc, left.at[l], clean, right.at[r])

    live_terms(own_codes, here, here, self_term)
    live_terms(own_codes, here, friend, lambda l, r: adjoint(acc, left.at[l], friend_clean, right.at[r]))
    live_terms(friend_codes, friend, here, lambda l, r: forward(acc, left.at[l], friend_clean, right.at[r]))


def picked(codes, owner, want, lefts, rights):
    live = jnp.int32(0)
    for k in range(codes.shape[0]):
        lefts[k] = 0
        rights[k] = 0
    for k in range(codes.shape[0]):
        lefts[live] = codes[k, 1] - 1
        rights[live] = codes[k, 2] - 1
        live += (owner + codes[k, 0] - 2 == want).astype(jnp.int32)
    return live


def written(values):
    lane = lax.broadcasted_iota(jnp.int32, (1, len(values)), 1)
    row = jnp.zeros((1, len(values)), jnp.int32)
    for i, value in enumerate(values):
        row = jnp.where(lane == i, value, row)
    return row


def far_kernel(mine, plan, other_codes, other_block, left, right, near, out, clean, acc, lefts, rights):
    here = lax.axis_index("sector")
    other = other_of(here)
    share = out.shape[0]
    slots = other_codes.shape[0]
    size, adjoints = plan[0, 0], plan[0, 2]
    clean[...] = cleaned(other_block[0], plan[0, 1])
    forwards = picked(other_codes, other, here, lefts, rights)

    def run(rows):
        first = rows.start or 0
        acc[...] = near[rows, :]

        def forward_left(i):
            return left[lefts[i], rows, :]

        def adjoint_left(i):
            return left[plan[0, 3 + i], :, rows]

        def adjoint_right(i):
            return right[plan[0, 3 + slots + i]]

        def forward_pair(i, carry):
            a = jnp.concatenate([forward_left(2 * i), forward_left(2 * i + 1)], axis=0)
            b = jnp.concatenate([right[rights[2 * i]], right[rights[2 * i + 1]]], axis=0)
            middle = dot(a, clean[...], 1, 0).astype(BF16)
            acc[...] += dot(jnp.concatenate([middle[:share], middle[share:]], axis=1), b, 1, 0)
            return carry

        def adjoint_pair(i, carry):
            a = jnp.concatenate([adjoint_left(2 * i), adjoint_left(2 * i + 1)], axis=1)
            b = jnp.concatenate([adjoint_right(2 * i), adjoint_right(2 * i + 1)], axis=1)
            middle = dot(a, clean[...], 0, 0).astype(BF16)
            acc[...] += dot(jnp.concatenate([middle[:share], middle[share:]], axis=1), b, 1, 1)
            return carry

        def forward_one():
            middle = dot(forward_left(forwards - 1), clean[...], 1, 0).astype(BF16)
            return dot(middle, right[rights[forwards - 1]], 1, 0)

        def adjoint_one():
            middle = dot(adjoint_left(adjoints - 1), clean[...], 0, 0).astype(BF16)
            return dot(middle, adjoint_right(adjoints - 1), 1, 1)

        @pl.when(first < size)
        def _():
            lax.fori_loop(0, forwards // 2, forward_pair, 0)
            lax.fori_loop(0, adjoints // 2, adjoint_pair, 0)
            rest_forward, rest_adjoint = forwards % 2 == 1, adjoints % 2 == 1

            @pl.when(rest_forward & rest_adjoint)
            def _():
                acc[...] += forward_one() + adjoint_one()

            @pl.when(rest_forward & ~rest_adjoint)
            def _():
                acc[...] += forward_one()

            @pl.when(rest_adjoint & ~rest_forward)
            def _():
                acc[...] += adjoint_one()

        out[...] = masked(acc[...], size, first).astype(out.dtype)

    if share == near.shape[0]:
        run(slice(None))
        return
    for g in range(near.shape[0] // share):
        @pl.when((lax.axis_index("group") == g) == mine)
        def _():
            run(slice(g * share, (g + 1) * share))


def last_kernel(kept, *refs):
    total = kept[...]
    for part in refs[:-1]:
        total = total + part[...].astype(F32)
    refs[-1][0] = total.astype(BF16)


def shards(wavefunction, left_factors, right_factors, term_list, term_counts, sector_sizes):
    width = wavefunction.shape[1]
    groups = lax.axis_size("group")
    sectors = lax.axis_size("sector")
    share = width // groups
    friends = [(s, friend_of(s)) for s in range(sectors) if friend_of(s) < sectors]
    others = [(s, other_of(s)) for s in range(sectors) if 0 <= other_of(s) < sectors]
    block = pltpu.VMEM((width, width), BF16)

    hbm = functools.partial(pltpu.with_memory_space_constraint, memory_space=pltpu.HBM)
    other_block = lax.ppermute(wavefunction, "sector", others)
    friend_block = lax.ppermute(wavefunction, "sector", friends)
    codes = pl.pallas_call(
        codes_kernel,
        out_shape=jax.ShapeDtypeStruct(term_list.shape, jnp.int32),
        in_specs=[VMEM, VMEM],
        out_specs=VMEM,
        compiler_params=pltpu.CompilerParams(vmem_limit_bytes=2**20),
        cost_estimate=pl.CostEstimate(flops=4 * 10**9, transcendentals=0, bytes_accessed=2**24),
        name="codes",
    )(hbm(term_list), term_counts[:, None])
    friend_codes = lax.ppermute(codes, "sector", friends)
    other_codes = lax.ppermute(codes, "sector", others)
    slots = term_list.shape[0]
    picks = pltpu.SMEM((slots,), jnp.int32)
    near, plan = pl.pallas_call(
        near_kernel,
        out_shape=[
            jax.ShapeDtypeStruct((width, width), F32),
            jax.ShapeDtypeStruct((1, 3 + 2 * slots), jnp.int32),
        ],
        in_specs=[SMEM, SMEM, SMEM, VMEM, VMEM, VMEM, VMEM],
        out_specs=[VMEM, VMEM],
        scratch_shapes=[block, block, picks, picks],
        compiler_params=PARAMS,
        name="near",
    )(codes, friend_codes, sector_sizes, wavefunction, friend_block, left_factors, right_factors)

    def far(rows, mine, dtype):
        return pl.pallas_call(
            functools.partial(far_kernel, mine),
            out_shape=jax.ShapeDtypeStruct((rows, width), dtype),
            in_specs=[SMEM, SMEM, VMEM, VMEM, VMEM, VMEM],
            out_specs=VMEM,
            scratch_shapes=[block, pltpu.VMEM((rows, width), F32), picks, picks],
            compiler_params=PARAMS,
            name="far_mine" if mine else "far_theirs",
        )(plan, other_codes, other_block, left_factors, right_factors, near)

    hops = [[(g, (g + hop) % groups) for g in range(groups)] for hop in range(1, groups)]
    if groups == 2 and share % 128 == 0:
        theirs = far(share, False, BF16)
        got = [lax.ppermute(theirs, "group", hops[0])]
        kept = far(share, True, F32)
    else:
        whole = far(width, True, F32)
        group = lax.axis_index("group")
        kept = lax.dynamic_slice_in_dim(whole, group * share, share, 0)
        got = []
        for hop, pairs in enumerate(hops, 1):
            part = lax.dynamic_slice_in_dim(whole, (group + hop) % groups * share, share, 0)
            got.append(lax.ppermute(part.astype(BF16), "group", pairs))
    return pl.pallas_call(
        last_kernel,
        out_shape=jax.ShapeDtypeStruct((1, share, width), BF16),
        in_specs=[VMEM] * (1 + len(got)),
        out_specs=VMEM,
        compiler_params=PARAMS,
        name="last",
    )(kept, *got)


def solution(mesh):
    return jax.shard_map(
        shards,
        mesh=mesh,
        in_specs=(
            P("sector", None, None),
            P("group", None, None),
            P("group", None, None),
            P(("group", "sector"), None),
            P(("group", "sector")),
            P(),
        ),
        out_specs=P("sector", "group", None),
        check_vma=False,
    )
```

```python
import functools

import jax
import jax.numpy as jnp
from jax import lax
from jax.experimental import pallas as pl
from jax.experimental.pallas import tpu as pltpu
from jax.sharding import PartitionSpec as P

F32 = jnp.float32
BF16 = jnp.bfloat16
VMEM = pl.BlockSpec(memory_space=pltpu.VMEM)
SMEM = pl.BlockSpec(memory_space=pltpu.SMEM)
PARAMS = pltpu.CompilerParams(vmem_limit_bytes=16 * 1024 * 1024)


def dot(a, b, ca, cb):
    return lax.dot_general(a, b, (((ca,), (cb,)), ((), ())), preferred_element_type=F32)


def forward(acc, left, source, right):
    middle = dot(left[...], source[...], 1, 0).astype(BF16)
    acc[...] += dot(middle, right[...], 1, 0)


def adjoint(acc, left, source, right):
    middle = dot(left[...], source[...], 0, 0).astype(BF16)
    acc[...] += dot(middle, right[...], 1, 1)


def friend_of(sector):
    return sector + 1 - 2 * (sector % 2)


def other_of(sector):
    return sector - 1 + 2 * (sector % 2)


def masked(block, size, first=0):
    rows = lax.broadcasted_iota(jnp.int32, block.shape, 0) + first
    cols = lax.broadcasted_iota(jnp.int32, block.shape, 1)
    return jnp.where((rows < size) & (cols < size), block, jnp.zeros_like(block))


def cleaned(block, size):
    rows = lax.broadcasted_iota(jnp.int32, (block.shape[0], 1), 0) < size
    cols = lax.broadcasted_iota(jnp.int32, (1, block.shape[1]), 1) < size
    return block * rows.astype(BF16) * cols.astype(BF16)


def live_terms(codes, owner, want, action):
    for k in range(codes.shape[0]):
        @pl.when(owner + codes[k, 0] - 2 == want)
        def _():
            action(codes[k, 1] - 1, codes[k, 2] - 1)


def codes_kernel(term_list, term_counts, codes):
    slot = lax.broadcasted_iota(jnp.int32, codes.shape, 0)
    codes[...] = jnp.where(slot < term_counts[...], term_list[...] + 1, 0)


def near_kernel(own_codes, friend_codes, sizes, own_block, friend_block, left, right,
                acc, plan, clean, friend_clean, lefts, rights):
    here = lax.axis_index("sector")
    friend = friend_of(here)
    other = other_of(here)
    slots = own_codes.shape[0]
    adjoints = picked(own_codes, here, other, lefts, rights)
    scalars = [sizes[here], sizes[jnp.clip(other, 0, sizes.shape[0] - 1)], adjoints]
    plan[...] = written(scalars + [lefts[k] for k in range(slots)] + [rights[k] for k in range(slots)])
    clean[...] = cleaned(own_block[0], sizes[here])
    friend_clean[...] = cleaned(friend_block[0], sizes[jnp.minimum(friend, sizes.shape[0] - 1)])
    acc[...] = jnp.zeros_like(acc)

    def self_term(l, r):
        forward(acc, left.at[l], clean, right.at[r])
        adjoint(acc, left.at[l], clean, right.at[r])

    live_terms(own_codes, here, here, self_term)
    live_terms(own_codes, here, friend, lambda l, r: adjoint(acc, left.at[l], friend_clean, right.at[r]))
    live_terms(friend_codes, friend, here, lambda l, r: forward(acc, left.at[l], friend_clean, right.at[r]))


def picked(codes, owner, want, lefts, rights):
    live = jnp.int32(0)
    for k in range(codes.shape[0]):
        lefts[k] = 0
        rights[k] = 0
    for k in range(codes.shape[0]):
        lefts[live] = codes[k, 1] - 1
        rights[live] = codes[k, 2] - 1
        live += (owner + codes[k, 0] - 2 == want).astype(jnp.int32)
    return live


def written(values):
    lane = lax.broadcasted_iota(jnp.int32, (1, len(values)), 1)
    row = jnp.zeros((1, len(values)), jnp.int32)
    for i, value in enumerate(values):
        row = jnp.where(lane == i, value, row)
    return row


def far_kernel(mine, plan, other_codes, other_block, left, right, near, out, clean, acc, lefts, rights):
    here = lax.axis_index("sector")
    other = other_of(here)
    share = out.shape[0]
    slots = other_codes.shape[0]
    size, adjoints = plan[0, 0], plan[0, 2]
    clean[...] = cleaned(other_block[0], plan[0, 1])
    forwards = picked(other_codes, other, here, lefts, rights)

    def run(rows):
        first = rows.start or 0
        acc[...] = near[rows, :]

        def forward_left(i):
            return left[lefts[i], rows, :]

        def adjoint_left(i):
            return left[plan[0, 3 + i], :, rows]

        def adjoint_right(i):
            return right[plan[0, 3 + slots + i]]

        def forward_pair(i, carry):
            a = jnp.concatenate([forward_left(2 * i), forward_left(2 * i + 1)], axis=0)
            b = jnp.concatenate([right[rights[2 * i]], right[rights[2 * i + 1]]], axis=0)
            middle = dot(a, clean[...], 1, 0).astype(BF16)
            acc[...] += dot(jnp.concatenate([middle[:share], middle[share:]], axis=1), b, 1, 0)
            return carry

        def adjoint_pair(i, carry):
            a = jnp.concatenate([adjoint_left(2 * i), adjoint_left(2 * i + 1)], axis=1)
            b = jnp.concatenate([adjoint_right(2 * i), adjoint_right(2 * i + 1)], axis=1)
            middle = dot(a, clean[...], 0, 0).astype(BF16)
            acc[...] += dot(jnp.concatenate([middle[:share], middle[share:]], axis=1), b, 1, 1)
            return carry

        def forward_one():
            middle = dot(forward_left(forwards - 1), clean[...], 1, 0).astype(BF16)
            return dot(middle, right[rights[forwards - 1]], 1, 0)

        def adjoint_one():
            middle = dot(adjoint_left(adjoints - 1), clean[...], 0, 0).astype(BF16)
            return dot(middle, adjoint_right(adjoints - 1), 1, 1)

        @pl.when(first < size)
        def _():
            lax.fori_loop(0, forwards // 2, forward_pair, 0)
            lax.fori_loop(0, adjoints // 2, adjoint_pair, 0)
            rest_forward, rest_adjoint = forwards % 2 == 1, adjoints % 2 == 1

            @pl.when(rest_forward & rest_adjoint)
            def _():
                acc[...] += forward_one() + adjoint_one()

            @pl.when(rest_forward & ~rest_adjoint)
            def _():
                acc[...] += forward_one()

            @pl.when(rest_adjoint & ~rest_forward)
            def _():
                acc[...] += adjoint_one()

        out[...] = masked(acc[...], size, first).astype(out.dtype)

    if share == near.shape[0]:
        run(slice(None))
        return
    for g in range(near.shape[0] // share):
        @pl.when((lax.axis_index("group") == g) == mine)
        def _():
            run(slice(g * share, (g + 1) * share))


def last_kernel(kept, *refs):
    parts, (out, ready, sems) = refs[:-3], refs[-3:]
    pieces = sems.shape[0]
    rows = kept.shape[0] // pieces
    copies = []
    for i in range(pieces):
        piece = slice(i * rows, (i + 1) * rows)
        total = kept[piece, :]
        for part in parts:
            total = total + part[piece, :].astype(F32)
        ready[piece, :] = total.astype(BF16)
        copies.append(pltpu.make_async_copy(ready.at[piece, :], out.at[0, piece, :], sems.at[i]))
        copies[-1].start()
    for copy in copies:
        copy.wait()


def shards(wavefunction, left_factors, right_factors, term_list, term_counts, sector_sizes):
    width = wavefunction.shape[1]
    groups = lax.axis_size("group")
    sectors = lax.axis_size("sector")
    share = width // groups
    friends = [(s, friend_of(s)) for s in range(sectors) if friend_of(s) < sectors]
    others = [(s, other_of(s)) for s in range(sectors) if 0 <= other_of(s) < sectors]
    block = pltpu.VMEM((width, width), BF16)

    hbm = functools.partial(pltpu.with_memory_space_constraint, memory_space=pltpu.HBM)
    other_block = lax.ppermute(wavefunction, "sector", others)
    friend_block = lax.ppermute(wavefunction, "sector", friends)
    codes = pl.pallas_call(
        codes_kernel,
        out_shape=jax.ShapeDtypeStruct(term_list.shape, jnp.int32),
        in_specs=[VMEM, VMEM],
        out_specs=VMEM,
        compiler_params=pltpu.CompilerParams(vmem_limit_bytes=2**20),
        cost_estimate=pl.CostEstimate(flops=4 * 10**9, transcendentals=0, bytes_accessed=2**24),
        name="codes",
    )(hbm(term_list), term_counts[:, None])
    friend_codes = lax.ppermute(codes, "sector", friends)
    other_codes = lax.ppermute(codes, "sector", others)
    slots = term_list.shape[0]
    picks = pltpu.SMEM((slots,), jnp.int32)
    near, plan = pl.pallas_call(
        near_kernel,
        out_shape=[
            jax.ShapeDtypeStruct((width, width), F32),
            jax.ShapeDtypeStruct((1, 3 + 2 * slots), jnp.int32),
        ],
        in_specs=[SMEM, SMEM, SMEM, VMEM, VMEM, VMEM, VMEM],
        out_specs=[VMEM, VMEM],
        scratch_shapes=[block, block, picks, picks],
        compiler_params=PARAMS,
        name="near",
    )(codes, friend_codes, sector_sizes, wavefunction, friend_block, left_factors, right_factors)

    def far(rows, mine, dtype):
        return pl.pallas_call(
            functools.partial(far_kernel, mine),
            out_shape=jax.ShapeDtypeStruct((rows, width), dtype),
            in_specs=[SMEM, SMEM, VMEM, VMEM, VMEM, VMEM],
            out_specs=VMEM,
            scratch_shapes=[block, pltpu.VMEM((rows, width), F32), picks, picks],
            compiler_params=PARAMS,
            name="far_mine" if mine else "far_theirs",
        )(plan, other_codes, other_block, left_factors, right_factors, near)

    hops = [[(g, (g + hop) % groups) for g in range(groups)] for hop in range(1, groups)]
    if groups == 2 and share % 128 == 0:
        theirs = far(share, False, BF16)
        got = [lax.ppermute(theirs, "group", hops[0])]
        kept = far(share, True, F32)
    else:
        whole = far(width, True, F32)
        group = lax.axis_index("group")
        kept = lax.dynamic_slice_in_dim(whole, group * share, share, 0)
        got = []
        for hop, pairs in enumerate(hops, 1):
            part = lax.dynamic_slice_in_dim(whole, (group + hop) % groups * share, share, 0)
            got.append(lax.ppermute(part.astype(BF16), "group", pairs))
    return pl.pallas_call(
        last_kernel,
        out_shape=jax.ShapeDtypeStruct((1, share, width), BF16),
        in_specs=[VMEM] * (1 + len(got)),
        out_specs=pl.BlockSpec(memory_space=pltpu.HBM),
        scratch_shapes=[pltpu.VMEM((share, width), BF16), pltpu.SemaphoreType.DMA((2,))],
        compiler_params=PARAMS,
        name="last",
    )(kept, *got)


def solution(mesh):
    return jax.shard_map(
        shards,
        mesh=mesh,
        in_specs=(
            P("sector", None, None),
            P("group", None, None),
            P("group", None, None),
            P(("group", "sector"), None),
            P(("group", "sector")),
            P(),
        ),
        out_specs=P("sector", "group", None),
        check_vma=False,
    )
```

```python
import functools

import jax
import jax.numpy as jnp
from jax import lax
from jax.experimental import pallas as pl
from jax.experimental.pallas import tpu as pltpu
from jax.sharding import PartitionSpec as P

F32 = jnp.float32
BF16 = jnp.bfloat16
VMEM = pl.BlockSpec(memory_space=pltpu.VMEM)
SMEM = pl.BlockSpec(memory_space=pltpu.SMEM)
PARAMS = pltpu.CompilerParams(vmem_limit_bytes=16 * 1024 * 1024)


def dot(a, b, ca, cb):
    return lax.dot_general(a, b, (((ca,), (cb,)), ((), ())), preferred_element_type=F32)


def forward(acc, left, source, right):
    middle = dot(left[...], source[...], 1, 0).astype(BF16)
    acc[...] += dot(middle, right[...], 1, 0)


def adjoint(acc, left, source, right):
    middle = dot(left[...], source[...], 0, 0).astype(BF16)
    acc[...] += dot(middle, right[...], 1, 1)


def friend_of(sector):
    return sector + 1 - 2 * (sector % 2)


def other_of(sector):
    return sector - 1 + 2 * (sector % 2)


def masked(block, size, first=0):
    rows = lax.broadcasted_iota(jnp.int32, block.shape, 0) + first
    cols = lax.broadcasted_iota(jnp.int32, block.shape, 1)
    return jnp.where((rows < size) & (cols < size), block, jnp.zeros_like(block))


def cleaned(block, size):
    rows = lax.broadcasted_iota(jnp.int32, (block.shape[0], 1), 0) < size
    cols = lax.broadcasted_iota(jnp.int32, (1, block.shape[1]), 1) < size
    return block * rows.astype(BF16) * cols.astype(BF16)


def live_terms(codes, owner, want, action):
    for k in range(codes.shape[0]):
        @pl.when(owner + codes[k, 0] - 2 == want)
        def _():
            action(codes[k, 1] - 1, codes[k, 2] - 1)


def codes_kernel(term_list, term_counts, codes):
    slot = lax.broadcasted_iota(jnp.int32, codes.shape, 0)
    codes[...] = jnp.where(slot < term_counts[...], term_list[...] + 1, 0)


def near_kernel(own_codes, friend_codes, sizes, own_block, friend_block, left, right,
                acc, plan, clean, friend_clean, lefts, rights):
    here = lax.axis_index("sector")
    friend = friend_of(here)
    other = other_of(here)
    slots = own_codes.shape[0]
    adjoints = picked(own_codes, here, other, lefts, rights)
    scalars = [sizes[here], sizes[jnp.clip(other, 0, sizes.shape[0] - 1)], adjoints]
    plan[...] = written(scalars + [lefts[k] for k in range(slots)] + [rights[k] for k in range(slots)])
    clean[...] = cleaned(own_block[0], sizes[here])
    friend_clean[...] = cleaned(friend_block[0], sizes[jnp.minimum(friend, sizes.shape[0] - 1)])
    acc[...] = jnp.zeros_like(acc)

    def self_term(l, r):
        forward(acc, left.at[l], clean, right.at[r])
        adjoint(acc, left.at[l], clean, right.at[r])

    live_terms(own_codes, here, here, self_term)
    live_terms(own_codes, here, friend, lambda l, r: adjoint(acc, left.at[l], friend_clean, right.at[r]))
    live_terms(friend_codes, friend, here, lambda l, r: forward(acc, left.at[l], friend_clean, right.at[r]))


def picked(codes, owner, want, lefts, rights):
    live = jnp.int32(0)
    for k in range(codes.shape[0]):
        lefts[k] = 0
        rights[k] = 0
    for k in range(codes.shape[0]):
        lefts[live] = codes[k, 1] - 1
        rights[live] = codes[k, 2] - 1
        live += (owner + codes[k, 0] - 2 == want).astype(jnp.int32)
    return live


def written(values):
    lane = lax.broadcasted_iota(jnp.int32, (1, len(values)), 1)
    row = jnp.zeros((1, len(values)), jnp.int32)
    for i, value in enumerate(values):
        row = jnp.where(lane == i, value, row)
    return row


def far_kernel(mine, plan, other_codes, other_block, left, right, near, out, clean, acc, lefts, rights):
    here = lax.axis_index("sector")
    other = other_of(here)
    share = out.shape[0]
    slots = other_codes.shape[0]
    size, adjoints = plan[0, 0], plan[0, 2]
    clean[...] = cleaned(other_block[0], plan[0, 1])
    forwards = picked(other_codes, other, here, lefts, rights)

    def run(rows):
        first = rows.start or 0
        acc[...] = near[rows, :]

        def forward_left(i):
            return left[lefts[i], rows, :]

        def adjoint_left(i):
            return left[plan[0, 3 + i], :, rows]

        def adjoint_right(i):
            return right[plan[0, 3 + slots + i]]

        def forward_pair(i, carry):
            a = jnp.concatenate([forward_left(2 * i), forward_left(2 * i + 1)], axis=0)
            b = jnp.concatenate([right[rights[2 * i]], right[rights[2 * i + 1]]], axis=0)
            middle = dot(a, clean[...], 1, 0).astype(BF16)
            acc[...] += dot(jnp.concatenate([middle[:share], middle[share:]], axis=1), b, 1, 0)
            return carry

        def adjoint_pair(i, carry):
            a = jnp.concatenate([adjoint_left(2 * i), adjoint_left(2 * i + 1)], axis=1)
            b = jnp.concatenate([adjoint_right(2 * i), adjoint_right(2 * i + 1)], axis=1)
            middle = dot(a, clean[...], 0, 0).astype(BF16)
            acc[...] += dot(jnp.concatenate([middle[:share], middle[share:]], axis=1), b, 1, 1)
            return carry

        def forward_one():
            middle = dot(forward_left(forwards - 1), clean[...], 1, 0).astype(BF16)
            return dot(middle, right[rights[forwards - 1]], 1, 0)

        def adjoint_one():
            middle = dot(adjoint_left(adjoints - 1), clean[...], 0, 0).astype(BF16)
            return dot(middle, adjoint_right(adjoints - 1), 1, 1)

        @pl.when(first < size)
        def _():
            lax.fori_loop(0, forwards // 2, forward_pair, 0)
            lax.fori_loop(0, adjoints // 2, adjoint_pair, 0)
            rest_forward, rest_adjoint = forwards % 2 == 1, adjoints % 2 == 1

            @pl.when(rest_forward & rest_adjoint)
            def _():
                a = jnp.concatenate([forward_left(forwards - 1), adjoint_left(adjoints - 1).T], axis=0)
                middle = dot(a, clean[...], 1, 0).astype(BF16)
                acc[...] += (dot(middle[:share], right[rights[forwards - 1]], 1, 0)
                             + dot(middle[share:], adjoint_right(adjoints - 1), 1, 1))

            @pl.when(rest_forward & ~rest_adjoint)
            def _():
                acc[...] += forward_one()

            @pl.when(rest_adjoint & ~rest_forward)
            def _():
                acc[...] += adjoint_one()

        out[...] = masked(acc[...], size, first).astype(out.dtype)

    if share == near.shape[0]:
        run(slice(None))
        return
    for g in range(near.shape[0] // share):
        @pl.when((lax.axis_index("group") == g) == mine)
        def _():
            run(slice(g * share, (g + 1) * share))


def last_kernel(kept, *refs):
    parts, (out, ready, sems) = refs[:-3], refs[-3:]
    pieces = sems.shape[0]
    rows = kept.shape[0] // pieces
    copies = []
    for i in range(pieces):
        piece = slice(i * rows, (i + 1) * rows)
        total = kept[piece, :]
        for part in parts:
            total = total + part[piece, :].astype(F32)
        ready[piece, :] = total.astype(BF16)
        copies.append(pltpu.make_async_copy(ready.at[piece, :], out.at[0, piece, :], sems.at[i]))
        copies[-1].start()
    for copy in copies:
        copy.wait()


def shards(wavefunction, left_factors, right_factors, term_list, term_counts, sector_sizes):
    width = wavefunction.shape[1]
    groups = lax.axis_size("group")
    sectors = lax.axis_size("sector")
    share = width // groups
    friends = [(s, friend_of(s)) for s in range(sectors) if friend_of(s) < sectors]
    others = [(s, other_of(s)) for s in range(sectors) if 0 <= other_of(s) < sectors]
    block = pltpu.VMEM((width, width), BF16)

    hbm = functools.partial(pltpu.with_memory_space_constraint, memory_space=pltpu.HBM)
    other_block = lax.ppermute(wavefunction, "sector", others)
    friend_block = lax.ppermute(wavefunction, "sector", friends)
    codes = pl.pallas_call(
        codes_kernel,
        out_shape=jax.ShapeDtypeStruct(term_list.shape, jnp.int32),
        in_specs=[VMEM, VMEM],
        out_specs=VMEM,
        compiler_params=pltpu.CompilerParams(vmem_limit_bytes=2**20),
        cost_estimate=pl.CostEstimate(flops=4 * 10**9, transcendentals=0, bytes_accessed=2**24),
        name="codes",
    )(hbm(term_list), term_counts[:, None])
    friend_codes = lax.ppermute(codes, "sector", friends)
    other_codes = lax.ppermute(codes, "sector", others)
    slots = term_list.shape[0]
    picks = pltpu.SMEM((slots,), jnp.int32)
    near, plan = pl.pallas_call(
        near_kernel,
        out_shape=[
            jax.ShapeDtypeStruct((width, width), F32),
            jax.ShapeDtypeStruct((1, 3 + 2 * slots), jnp.int32),
        ],
        in_specs=[SMEM, SMEM, SMEM, VMEM, VMEM, VMEM, VMEM],
        out_specs=[VMEM, VMEM],
        scratch_shapes=[block, block, picks, picks],
        compiler_params=PARAMS,
        name="near",
    )(codes, friend_codes, sector_sizes, wavefunction, friend_block, left_factors, right_factors)

    def far(rows, mine, dtype):
        return pl.pallas_call(
            functools.partial(far_kernel, mine),
            out_shape=jax.ShapeDtypeStruct((rows, width), dtype),
            in_specs=[SMEM, SMEM, VMEM, VMEM, VMEM, VMEM],
            out_specs=VMEM,
            scratch_shapes=[block, pltpu.VMEM((rows, width), F32), picks, picks],
            compiler_params=PARAMS,
            name="far_mine" if mine else "far_theirs",
        )(plan, other_codes, other_block, left_factors, right_factors, near)

    hops = [[(g, (g + hop) % groups) for g in range(groups)] for hop in range(1, groups)]
    if groups == 2 and share % 128 == 0:
        theirs = far(share, False, BF16)
        got = [lax.ppermute(theirs, "group", hops[0])]
        kept = far(share, True, F32)
    else:
        whole = far(width, True, F32)
        group = lax.axis_index("group")
        kept = lax.dynamic_slice_in_dim(whole, group * share, share, 0)
        got = []
        for hop, pairs in enumerate(hops, 1):
            part = lax.dynamic_slice_in_dim(whole, (group + hop) % groups * share, share, 0)
            got.append(lax.ppermute(part.astype(BF16), "group", pairs))
    return pl.pallas_call(
        last_kernel,
        out_shape=jax.ShapeDtypeStruct((1, share, width), BF16),
        in_specs=[VMEM] * (1 + len(got)),
        out_specs=pl.BlockSpec(memory_space=pltpu.HBM),
        scratch_shapes=[pltpu.VMEM((share, width), BF16), pltpu.SemaphoreType.DMA((2,))],
        compiler_params=PARAMS,
        name="last",
    )(kept, *got)


def solution(mesh):
    return jax.shard_map(
        shards,
        mesh=mesh,
        in_specs=(
            P("sector", None, None),
            P("group", None, None),
            P("group", None, None),
            P(("group", "sector"), None),
            P(("group", "sector")),
            P(),
        ),
        out_specs=P("sector", "group", None),
        check_vma=False,
    )
```

```python
import functools

import jax
import jax.numpy as jnp
from jax import lax
from jax.experimental import pallas as pl
from jax.experimental.pallas import tpu as pltpu
from jax.sharding import PartitionSpec as P

F32 = jnp.float32
BF16 = jnp.bfloat16
VMEM = pl.BlockSpec(memory_space=pltpu.VMEM)
SMEM = pl.BlockSpec(memory_space=pltpu.SMEM)
PARAMS = pltpu.CompilerParams(vmem_limit_bytes=16 * 1024 * 1024)


def dot(a, b, ca, cb):
    return lax.dot_general(a, b, (((ca,), (cb,)), ((), ())), preferred_element_type=F32)


def forward(acc, left, source, right):
    middle = dot(left[...], source[...], 1, 0).astype(BF16)
    acc[...] += dot(middle, right[...], 1, 0)


def adjoint(acc, left, source, right):
    middle = dot(left[...], source[...], 0, 0).astype(BF16)
    acc[...] += dot(middle, right[...], 1, 1)


def friend_of(sector):
    return sector + 1 - 2 * (sector % 2)


def other_of(sector):
    return sector - 1 + 2 * (sector % 2)


def masked(block, size, first=0):
    rows = lax.broadcasted_iota(jnp.int32, block.shape, 0) + first
    cols = lax.broadcasted_iota(jnp.int32, block.shape, 1)
    return jnp.where((rows < size) & (cols < size), block, jnp.zeros_like(block))


def cleaned(block, size):
    rows = lax.broadcasted_iota(jnp.int32, (block.shape[0], 1), 0) < size
    cols = lax.broadcasted_iota(jnp.int32, (1, block.shape[1]), 1) < size
    return block * rows.astype(BF16) * cols.astype(BF16)


def live_terms(codes, owner, want, action):
    for k in range(codes.shape[0]):
        @pl.when(owner + codes[k, 0] - 2 == want)
        def _():
            action(codes[k, 1] - 1, codes[k, 2] - 1)


def codes_kernel(term_list, term_counts, codes):
    slot = lax.broadcasted_iota(jnp.int32, codes.shape, 0)
    codes[...] = jnp.where(slot < term_counts[...], term_list[...] + 1, 0)


def near_kernel(own_codes, friend_codes, sizes, own_block, friend_block, left, right,
                acc, plan, left_turned, right_turned, clean, friend_clean, lefts, rights):
    here = lax.axis_index("sector")
    friend = friend_of(here)
    other = other_of(here)
    slots = own_codes.shape[0]
    adjoints = picked(own_codes, here, other, lefts, rights)
    scalars = [sizes[here], sizes[jnp.clip(other, 0, sizes.shape[0] - 1)], adjoints]
    plan[...] = written(scalars + [lefts[k] for k in range(slots)] + [rights[k] for k in range(slots)])
    clean[...] = cleaned(own_block[0], sizes[here])
    friend_clean[...] = cleaned(friend_block[0], sizes[jnp.minimum(friend, sizes.shape[0] - 1)])
    acc[...] = jnp.zeros_like(acc)

    def self_term(l, r):
        forward(acc, left.at[l], clean, right.at[r])
        adjoint(acc, left.at[l], clean, right.at[r])

    live_terms(own_codes, here, here, self_term)
    live_terms(own_codes, here, friend, lambda l, r: adjoint(acc, left.at[l], friend_clean, right.at[r]))
    live_terms(friend_codes, friend, here, lambda l, r: forward(acc, left.at[l], friend_clean, right.at[r]))

    def turn(i, carry):
        left_turned[i] = left[lefts[i]].T
        right_turned[i] = right[rights[i]].T
        return carry

    lax.fori_loop(0, adjoints, turn, 0)


def picked(codes, owner, want, lefts, rights):
    live = jnp.int32(0)
    for k in range(codes.shape[0]):
        lefts[k] = 0
        rights[k] = 0
    for k in range(codes.shape[0]):
        lefts[live] = codes[k, 1] - 1
        rights[live] = codes[k, 2] - 1
        live += (owner + codes[k, 0] - 2 == want).astype(jnp.int32)
    return live


def written(values):
    lane = lax.broadcasted_iota(jnp.int32, (1, len(values)), 1)
    row = jnp.zeros((1, len(values)), jnp.int32)
    for i, value in enumerate(values):
        row = jnp.where(lane == i, value, row)
    return row


def far_kernel(mine, plan, other_codes, other_block, left, right, left_turned, right_turned, near, out,
               clean, acc, lefts, rights):
    here = lax.axis_index("sector")
    other = other_of(here)
    share = out.shape[0]
    size, adjoints = plan[0, 0], plan[0, 2]
    clean[...] = cleaned(other_block[0], plan[0, 1])
    forwards = picked(other_codes, other, here, lefts, rights)

    def run(first):
        rows = pl.ds(first, share)
        acc[...] = near[rows, :]

        def forward_left(i):
            return left[lefts[i], rows, :]

        def adjoint_left(i):
            return left_turned[i, rows, :]

        def adjoint_right(i):
            return right_turned[i]

        def forward_pair(i, carry):
            a = jnp.concatenate([forward_left(2 * i), forward_left(2 * i + 1)], axis=0)
            b = jnp.concatenate([right[rights[2 * i]], right[rights[2 * i + 1]]], axis=0)
            middle = dot(a, clean[...], 1, 0).astype(BF16)
            acc[...] += dot(jnp.concatenate([middle[:share], middle[share:]], axis=1), b, 1, 0)
            return carry

        def adjoint_pair(i, carry):
            a = jnp.concatenate([adjoint_left(2 * i), adjoint_left(2 * i + 1)], axis=0)
            b = jnp.concatenate([adjoint_right(2 * i), adjoint_right(2 * i + 1)], axis=0)
            middle = dot(a, clean[...], 1, 0).astype(BF16)
            acc[...] += dot(jnp.concatenate([middle[:share], middle[share:]], axis=1), b, 1, 0)
            return carry

        def forward_one():
            middle = dot(forward_left(forwards - 1), clean[...], 1, 0).astype(BF16)
            return dot(middle, right[rights[forwards - 1]], 1, 0)

        def adjoint_one():
            middle = dot(adjoint_left(adjoints - 1), clean[...], 1, 0).astype(BF16)
            return dot(middle, adjoint_right(adjoints - 1), 1, 0)

        @pl.when(first < size)
        def _():
            lax.fori_loop(0, forwards // 2, forward_pair, 0)
            lax.fori_loop(0, adjoints // 2, adjoint_pair, 0)
            rest_forward, rest_adjoint = forwards % 2 == 1, adjoints % 2 == 1

            @pl.when(rest_forward & rest_adjoint)
            def _():
                a = jnp.concatenate([forward_left(forwards - 1), adjoint_left(adjoints - 1)], axis=0)
                b = jnp.concatenate([right[rights[forwards - 1]], adjoint_right(adjoints - 1)], axis=0)
                middle = dot(a, clean[...], 1, 0).astype(BF16)
                acc[...] += dot(jnp.concatenate([middle[:share], middle[share:]], axis=1), b, 1, 0)

            @pl.when(rest_forward & ~rest_adjoint)
            def _():
                acc[...] += forward_one()

            @pl.when(rest_adjoint & ~rest_forward)
            def _():
                acc[...] += adjoint_one()

        out[...] = masked(acc[...], size, first).astype(out.dtype)

    groups = near.shape[0] // share
    group = lax.axis_index("group")
    run(pl.multiple_of((group if mine else groups - 1 - group) * share, share) if groups > 1 else 0)


def last_kernel(kept, *refs):
    parts, (out, ready, sems) = refs[:-3], refs[-3:]
    pieces = sems.shape[0]
    rows = kept.shape[0] // pieces
    copies = []
    for i in range(pieces):
        piece = slice(i * rows, (i + 1) * rows)
        total = kept[piece, :]
        for part in parts:
            total = total + part[piece, :].astype(F32)
        ready[piece, :] = total.astype(BF16)
        copies.append(pltpu.make_async_copy(ready.at[piece, :], out.at[0, piece, :], sems.at[i]))
        copies[-1].start()
    for copy in copies:
        copy.wait()


def shards(wavefunction, left_factors, right_factors, term_list, term_counts, sector_sizes):
    width = wavefunction.shape[1]
    groups = lax.axis_size("group")
    sectors = lax.axis_size("sector")
    share = width // groups
    friends = [(s, friend_of(s)) for s in range(sectors) if friend_of(s) < sectors]
    others = [(s, other_of(s)) for s in range(sectors) if 0 <= other_of(s) < sectors]
    block = pltpu.VMEM((width, width), BF16)

    hbm = functools.partial(pltpu.with_memory_space_constraint, memory_space=pltpu.HBM)
    other_block = lax.ppermute(wavefunction, "sector", others)
    friend_block = lax.ppermute(wavefunction, "sector", friends)
    codes = pl.pallas_call(
        codes_kernel,
        out_shape=jax.ShapeDtypeStruct(term_list.shape, jnp.int32),
        in_specs=[VMEM, VMEM],
        out_specs=VMEM,
        compiler_params=pltpu.CompilerParams(vmem_limit_bytes=2**20),
        cost_estimate=pl.CostEstimate(flops=4 * 10**9, transcendentals=0, bytes_accessed=2**24),
        name="codes",
    )(hbm(term_list), term_counts[:, None])
    friend_codes = lax.ppermute(codes, "sector", friends)
    other_codes = lax.ppermute(codes, "sector", others)
    slots = term_list.shape[0]
    picks = pltpu.SMEM((slots,), jnp.int32)
    near, plan, left_turned, right_turned = pl.pallas_call(
        near_kernel,
        out_shape=[
            jax.ShapeDtypeStruct((width, width), F32),
            jax.ShapeDtypeStruct((1, 3 + 2 * slots), jnp.int32),
            jax.ShapeDtypeStruct((slots, width, width), BF16),
            jax.ShapeDtypeStruct((slots, width, width), BF16),
        ],
        in_specs=[SMEM, SMEM, SMEM, VMEM, VMEM, VMEM, VMEM],
        out_specs=[VMEM] * 4,
        scratch_shapes=[block, block, picks, picks],
        compiler_params=PARAMS,
        name="near",
    )(codes, friend_codes, sector_sizes, wavefunction, friend_block, left_factors, right_factors)

    def far(rows, mine, dtype):
        return pl.pallas_call(
            functools.partial(far_kernel, mine),
            out_shape=jax.ShapeDtypeStruct((rows, width), dtype),
            in_specs=[SMEM, SMEM] + [VMEM] * 6,
            out_specs=VMEM,
            scratch_shapes=[block, pltpu.VMEM((rows, width), F32), picks, picks],
            compiler_params=PARAMS,
            name="far_mine" if mine else "far_theirs",
        )(plan, other_codes, other_block, left_factors, right_factors, left_turned, right_turned, near)

    hops = [[(g, (g + hop) % groups) for g in range(groups)] for hop in range(1, groups)]
    if groups == 2 and share % 128 == 0:
        theirs = far(share, False, BF16)
        got = [lax.ppermute(theirs, "group", hops[0])]
        kept = far(share, True, F32)
    else:
        whole = far(width, True, F32)
        group = lax.axis_index("group")
        kept = lax.dynamic_slice_in_dim(whole, group * share, share, 0)
        got = []
        for hop, pairs in enumerate(hops, 1):
            part = lax.dynamic_slice_in_dim(whole, (group + hop) % groups * share, share, 0)
            got.append(lax.ppermute(part.astype(BF16), "group", pairs))
    return pl.pallas_call(
        last_kernel,
        out_shape=jax.ShapeDtypeStruct((1, share, width), BF16),
        in_specs=[VMEM] * (1 + len(got)),
        out_specs=pl.BlockSpec(memory_space=pltpu.HBM),
        scratch_shapes=[pltpu.VMEM((share, width), BF16), pltpu.SemaphoreType.DMA((4,))],
        compiler_params=PARAMS,
        name="last",
    )(kept, *got)


def solution(mesh):
    return jax.shard_map(
        shards,
        mesh=mesh,
        in_specs=(
            P("sector", None, None),
            P("group", None, None),
            P("group", None, None),
            P(("group", "sector"), None),
            P(("group", "sector")),
            P(),
        ),
        out_specs=P("sector", "group", None),
        check_vma=False,
    )
```
